32 devices in a mesh: cells: 8 (over y, x, core), grp: 4 (over z).
Axes of the slice: x: 2, y: 2, z: 4, core: 2. Of those that a mesh axis runs over, the one named last changes fastest.
Arguments:
- fraction: float32 [3, 8, 4, 512], P(None, 'cells', 'grp'), may hold values from 0 to 1
- velocity: float32 [3, 8, 4, 512], P(None, 'cells', 'grp'), may hold values from -1.8 to 1.8
- anchor: int32 [3, 8, 4, 512], P(None, 'cells', 'grp'), may hold values from 0 to 254, as said below
- atom_types: int32 [8, 4, 512], P('cells', 'grp'), may hold values from 0 to 7
- counts: int32 [8, 4], P('cells', 'grp'), may hold values from 64 to 512, as said below
- type_table: float32 [3, 8], replicated, may hold values from 0.7 to 2.8, as said below
- target: float32 [32, 64, 256], P('cells', 'grp'), may hold values from -0.3 to 0.3
Outputs:
- final_velocity: float32 [3, 8, 4, 512], P(None, 'cells', 'grp')
- displacement: float32 [3, 8, 4, 512], P(None, 'cells', 'grp')
- potential: float32 [32, 64, 256], P('cells', 'grp')
The draws below stay inside these ranges and needn't reach their ends.
Inputs may be any that keep to these rules, and one draw needn't show every extreme that they name: `counts`: some cell holds exactly 512 live atoms in every draw; dead slots follow the live ones. `anchor`: component 0 is below 4, component 1 below 16, component 2 below 255. `type_table`: all entries are positive.
All inputs are finite; a program needn't handle non-finite values.
Results may differ from the reference program's by a relative error of at most 0.0003.
Values sent between devices are 32-bit elements; how exact they have to be, the bound alone decides.
A program may use at most 64 MiB of HBM per device.

```python
import jax
import jax.numpy as jnp
from jax import lax

BX = 4
BYD = 16
GZ = 256
ATOM_DEV = 512
TYPES = 8
STEPS = 2
NX = 32
NY = 64
N_CELLS = 8
N_GRP = 4


def draw_counts(key, part):
    first_key, second_key = jax.random.split(jax.random.fold_in(key, 11))
    levels = jax.random.randint(first_key, (N_CELLS, N_GRP), 0, 4, dtype=jnp.int32)
    values = (ATOM_DEV // jnp.power(jnp.int32(2), levels)).astype(jnp.int32)
    chosen = jax.random.randint(second_key, (), 0, N_CELLS * N_GRP, dtype=jnp.int32)
    values = values.reshape(-1).at[chosen].set(ATOM_DEV).reshape(N_CELLS, N_GRP)
    return values.astype(jnp.int32)


def draw_anchor(key, part):
    base_key = jax.random.fold_in(key, 23)
    raw_key, band_key, phase_key, pick_key, spare_key, chosen_key = jax.random.split(base_key, 6)
    raw_values = jax.random.randint(raw_key, (3, N_CELLS, N_GRP, ATOM_DEV), 0, 1048576, dtype=jnp.int32)
    band_width = min(24, GZ // 2)
    swing_depth = min(16, GZ - 1 - band_width)
    band_base = jax.random.randint(band_key, (), 0, GZ - band_width - swing_depth, dtype=jnp.int32)
    phase_shift = jax.random.randint(phase_key, (), 0, 2 * swing_depth, dtype=jnp.int32)
    cell_rows = jnp.arange(N_CELLS, dtype=jnp.int32)[:, None]
    cell_columns = jnp.arange(N_GRP, dtype=jnp.int32)[None, :]
    triangle = jnp.abs((cell_rows + cell_columns + phase_shift) % (2 * swing_depth) - swing_depth)
    in_band = band_base + triangle[:, :, None] + raw_values[2] % band_width
    background = jax.random.randint(spare_key, (N_CELLS, N_GRP, ATOM_DEV), 0, GZ - 1, dtype=jnp.int32)
    picked = jax.random.randint(pick_key, (N_CELLS, N_GRP, ATOM_DEV), 0, 8, dtype=jnp.int32) == 0
    depth_values = jnp.where(picked, background, in_band)
    chosen = jax.random.randint(chosen_key, (), 0, N_CELLS * N_GRP, dtype=jnp.int32)
    depth_values = depth_values.reshape(N_CELLS * N_GRP, ATOM_DEV).at[chosen, 0].set(GZ - 2).reshape(N_CELLS, N_GRP, ATOM_DEV)
    first_values = raw_values[0] % BX
    second_values = raw_values[1] % BYD
    return jnp.stack([first_values, second_values, depth_values]).astype(jnp.int32)


def draw_type_table(key, part):
    amp_key, width_key, mass_key = jax.random.split(jax.random.fold_in(key, 37), 3)
    amplitude = jnp.exp(jax.random.uniform(amp_key, (TYPES,), jnp.float32, jnp.log(0.7), jnp.log(2.0)))
    widths = jax.random.uniform(width_key, (TYPES,), jnp.float32, 1.7, 2.4)
    masses = jnp.exp(jax.random.uniform(mass_key, (TYPES,), jnp.float32, jnp.log(0.7), jnp.log(2.0)))
    return jnp.stack([amplitude, widths, masses]).astype(jnp.float32)


def set_ends(values, own_key, low, top_value):
    place = [jax.random.randint(jax.random.fold_in(own_key, axis), (), 0, length) for axis, length in enumerate(values.shape)]
    widest = values.shape.index(max(values.shape))
    neighbour = place[:widest] + [(place[widest] + 1) % values.shape[widest]] + place[widest + 1:]
    return values.at[tuple(place)].set(low).at[tuple(neighbour)].set(top_value)


def steps_of(key, shape, shards, low, high):
    factor_of = 1.0
    for dim, shards_of in shards:
        draws = jax.random.uniform(jax.random.fold_in(jax.random.fold_in(key, 6), dim), (shards_of,), jnp.float32, low / len(shards), high / len(shards))
        factor_of = factor_of * jnp.repeat(jnp.exp(draws), shape[dim] // shards_of).reshape((-1,) + (1,) * (len(shape) - 1 - dim))
    return factor_of


def gaussian(stream_key, dims, deviation, limit, cuts=(), kind=jnp.bfloat16):
    values = deviation * jax.random.normal(stream_key, dims, jnp.float32)
    if cuts:
        values = values * steps_of(stream_key, dims, cuts, -0.22, 0.18)
    return jnp.clip(values, -limit, limit).astype(kind)


def setup_inputs(seed: int = 0) -> dict:
    keys = jax.random.split(jax.random.key(seed), 8)
    return {
        "fraction": jnp.clip(1.0 * jax.random.uniform(keys[0], (3, N_CELLS, N_GRP, ATOM_DEV), jnp.float32) ** steps_of(keys[0], (3, N_CELLS, N_GRP, ATOM_DEV), ((1, 8), (2, 4)), -0.2, 0.2), 0.0, 1.0),
        "velocity": gaussian(keys[1], (3, N_CELLS, N_GRP, ATOM_DEV), 0.3, 1.8, ((1, 8), (2, 4)), jnp.float32),
        "anchor": draw_anchor(jax.random.fold_in(keys[7], 71), 0),
        "atom_types": set_ends(jax.random.randint(keys[3], (N_CELLS, N_GRP, ATOM_DEV), 0, TYPES), jax.random.fold_in(keys[3], 1), 0, TYPES - 1).astype(jnp.int32),
        "counts": draw_counts(jax.random.fold_in(keys[7], 71), 0),
        "type_table": draw_type_table(jax.random.fold_in(keys[7], 71), 0),
        "target": gaussian(keys[6], (NX, NY, GZ), 0.05, 0.3, ((0, 8), (1, 4)), jnp.float32),
    }


EPSILON = 1e-06
TIME_STEP = 0.5
BLUR_KERNEL = (1.0 / 16.0, 4.0 / 16.0, 6.0 / 16.0, 4.0 / 16.0, 1.0 / 16.0)
BOX_KERNEL = (1.0 / 9.0,) * 9

def tap_valid(values, along_axis, kernel):
    radius = (len(kernel) - 1) // 2
    length = values.shape[along_axis] - 2 * radius
    summed = kernel[0] * lax.slice_in_dim(values, 0, length, axis=along_axis)
    for offset in range(1, len(kernel)):
        summed = summed + kernel[offset] * lax.slice_in_dim(values, offset, offset + length, axis=along_axis)
    return summed

def tap_padded(values, along_axis, kernel):
    radius = (len(kernel) - 1) // 2
    widths = [(0, 0)] * values.ndim
    widths[along_axis] = (radius, radius)
    return tap_valid(jnp.pad(values, widths), along_axis, kernel)

def filter_three(values, kernel):
    return tap_padded(tap_padded(tap_padded(values, 0, kernel), 1, kernel), 2, kernel)

def corner_weights(position, fraction, extent):
    places = jnp.arange(extent, dtype=jnp.float32)
    lower = (position[:, None] == places[None, :]).astype(jnp.float32)
    upper = (position[:, None] + 1.0 == places[None, :]).astype(jnp.float32)
    return (lower * (1.0 - fraction[:, None]) + upper * fraction[:, None], upper - lower)

def spread_brick(anchors, fractions, amounts, extent_x, extent_y, extent_z):
    atom_count = anchors.shape[1]
    weight_x = corner_weights(anchors[0], fractions[0], extent_x)[0]
    weight_y = corner_weights(anchors[1], fractions[1], extent_y)[0]
    weight_z = corner_weights(anchors[2], fractions[2], extent_z)[0]
    plane = (weight_x[:, :, None] * weight_y[:, None, :]).reshape(atom_count, extent_x * extent_y)
    depth = weight_z * amounts[:, None]
    summed = lax.dot_general(plane, depth, (((0,), (0,)), ((), ())), precision=lax.Precision.HIGHEST, preferred_element_type=jnp.float32)
    return summed.reshape(extent_x, extent_y, extent_z)

def sample_gradient(anchors, fractions, field):
    extent_x, extent_y, extent_z = field.shape
    atom_count = anchors.shape[1]
    weight_x, slope_x = corner_weights(anchors[0], fractions[0], extent_x)
    weight_y, slope_y = corner_weights(anchors[1], fractions[1], extent_y)
    weight_z, slope_z = corner_weights(anchors[2], fractions[2], extent_z)
    matrix = field.reshape(extent_x * extent_y, extent_z)
    stacked = jnp.concatenate([weight_z, slope_z], 0)
    product = lax.dot_general(stacked, matrix, (((1,), (1,)), ((), ())), precision=lax.Precision.HIGHEST, preferred_element_type=jnp.float32)
    product = product.reshape(2, atom_count, extent_x, extent_y)
    grad_x = jnp.einsum('ax,ay,axy->a', slope_x, weight_y, product[0], precision=lax.Precision.HIGHEST)
    grad_y = jnp.einsum('ax,ay,axy->a', weight_x, slope_y, product[0], precision=lax.Precision.HIGHEST)
    grad_z = jnp.einsum('ax,ay,axy->a', weight_x, weight_y, product[1], precision=lax.Precision.HIGHEST)
    return jnp.stack([grad_x, grad_y, grad_z])

def pair_block(own, others):
    offsets = own[0:3, :, None] - others[0:3, None, :] + (own[3:6, :, None] - others[3:6, None, :])
    distance = lax.optimization_barrier(jnp.sum(offsets * offsets, 0))
    spread = own[7][:, None] + others[7][None, :]
    coupling = others[6][None, :] * jnp.exp(-0.5 * distance / spread) / spread
    return own[6][None, :] * lax.optimization_barrier(jnp.sum(coupling[None] * offsets, 2))

def type_values(kinds, table):
    matches = (kinds[..., None] == jnp.arange(table.shape[1], dtype=jnp.int32)).astype(jnp.float32)
    shaped = table.reshape((3,) + (1,) * kinds.ndim + (table.shape[1],))
    return lax.optimization_barrier(jnp.sum(matches[None] * shaped, -1))

def cell_pairs(own, others):
    block_size = min(128, own.shape[1])
    blocks = own.reshape(8, -1, block_size).transpose(1, 0, 2)
    result = lax.map(lambda piece: pair_block(piece, others), blocks)
    return result.transpose(1, 0, 2).reshape(3, -1)

def all_pairs(packet):
    padded = jnp.pad(packet, ((0, 0), (1, 1), (1, 1), (0, 0)))

    def per_slab(slab_index):
        window = lax.dynamic_slice(padded, (jnp.int32(0), slab_index, jnp.int32(0), jnp.int32(0)), (8, 3, N_GRP + 2, ATOM_DEV))
        pieces = []
        for quarter in range(N_GRP):
            others = window[:, :, quarter:quarter + 3, :].reshape(8, 9 * ATOM_DEV)
            pieces.append(cell_pairs(window[:, 1, quarter + 1, :], others))
        return jnp.stack(pieces, 1)
    result = lax.map(per_slab, jnp.arange(N_CELLS, dtype=jnp.int32))
    return result.transpose(1, 0, 2, 3)

def full_density(anchor_local, fraction, charge):

    def per_slab(inputs):
        anchors, fractions, amounts = inputs
        return jnp.stack([spread_brick(anchors[:, quarter], fractions[:, quarter], amounts[quarter], BX + 1, BYD + 1, GZ) for quarter in range(N_GRP)])
    bricks = lax.map(per_slab, (jnp.moveaxis(anchor_local, 1, 0), jnp.moveaxis(fraction, 1, 0), charge))
    rows_out = bricks[:, :, BX]
    arrived = jnp.concatenate([jnp.zeros_like(rows_out[:1]), rows_out[:-1]], 0)
    upper = bricks[:, :, :BX].at[:, :, 0].add(arrived)
    columns = upper[:, :, :, BYD]
    arrived_side = jnp.concatenate([jnp.zeros_like(columns[:, :1]), columns[:, :-1]], 1)
    inner = upper[:, :, :, :BYD].at[:, :, :, 0].add(arrived_side)
    return inner.transpose(0, 2, 1, 3, 4).reshape(NX, NY, GZ)

def full_gradient(anchor_local, fraction, field):
    padded = jnp.pad(field, ((0, 1), (0, 1), (0, 0)))

    def per_slab(inputs):
        slab_index, anchors, fractions = inputs
        planes = lax.dynamic_slice_in_dim(padded, slab_index * BX, BX + 1, 0)
        return jnp.stack([sample_gradient(anchors[:, quarter], fractions[:, quarter], planes[:, quarter * BYD:quarter * BYD + BYD + 1]) for quarter in range(N_GRP)], 1)
    result = lax.map(per_slab, (jnp.arange(N_CELLS, dtype=jnp.int32), jnp.moveaxis(anchor_local, 1, 0), jnp.moveaxis(fraction, 1, 0)))
    return result.transpose(1, 0, 2, 3)

def reference(fraction, velocity, anchor, atom_types, counts, type_table, target):
    live = (jnp.arange(ATOM_DEV, dtype=jnp.int32)[None, None, :] < counts[:, :, None]).astype(jnp.float32)
    properties = type_values(atom_types, type_table)
    charge = properties[0] * live
    square_width = properties[1] * properties[1]
    masses = properties[2]
    first_x = jnp.broadcast_to((jnp.arange(N_CELLS, dtype=jnp.int32) * BX)[:, None], (N_CELLS, N_GRP))
    first_y = jnp.broadcast_to((jnp.arange(N_GRP, dtype=jnp.int32) * BYD)[None, :], (N_CELLS, N_GRP))
    root = jnp.stack([first_x, first_y, jnp.zeros((N_CELLS, N_GRP), jnp.int32)])
    anchor_local = anchor.astype(jnp.float32)
    anchor_global = (anchor + root[..., None]).astype(jnp.float32)
    mean_one = filter_three(target, BOX_KERNEL)
    mean_two = filter_three(target * target, BOX_KERNEL)
    inverse_scale = lax.rsqrt(mean_two - mean_one * mean_one + EPSILON)
    moved = jnp.zeros_like(velocity)
    potential = jnp.zeros_like(target)
    for turn_index in range(STEPS):
        packet = jnp.concatenate([anchor_global, fraction, charge[None], square_width[None]], 0)
        forces = all_pairs(packet)
        density = full_density(anchor_local, fraction, charge)
        residual = (filter_three(density, BLUR_KERNEL) - target) * inverse_scale
        potential = filter_three(residual, BLUR_KERNEL)
        gradient = full_gradient(anchor_local, fraction, potential)
        forces = forces - charge[None] * gradient
        velocity = velocity + TIME_STEP * forces / masses[None]
        moved = moved + TIME_STEP * velocity
        fraction = fraction + TIME_STEP * velocity
    return (velocity * live[None], moved * live[None], potential)
```

```python
import functools
import math

import jax
import jax.numpy as jnp
from jax import lax
from jax.experimental import pallas as pl
from jax.experimental.pallas import tpu as pltpu
from jax.sharding import PartitionSpec as P

EPSILON = 1e-06
TIME_STEP = 0.5
TAPS = (1.0 / 16.0, 4.0 / 16.0, 6.0 / 16.0, 4.0 / 16.0, 1.0 / 16.0)
F32 = jnp.float32
BF16 = jnp.bfloat16
RX, RY = 2, 1
NB = 2 * RY + 1
SLOTS = (2 * RX + 1) * NB
OWN = RX * NB + RY
MESH = pl.DeviceIdType.MESH
VMEM = pl.BlockSpec(memory_space=pltpu.VMEM)
SMEM = pl.BlockSpec(memory_space=pltpu.SMEM)
ANY = pl.BlockSpec(memory_space=pl.ANY)
NEIGHBOURS = tuple(
    (a, b) for a in range(-RX, RX + 1) for b in range(-RY, RY + 1) if (a, b) != (0, 0)
)


def slot_of(a, b):
    return (a + RX) * NB + (b + RY)


def exists(a, b):
    s = lax.axis_index("cells") + a
    q = lax.axis_index("grp") + b
    ns, nq = lax.axis_size("cells"), lax.axis_size("grp")
    return (s >= 0) & (s < ns) & (q >= 0) & (q < nq)


def target_piece(a, b, bx, by):
    x0 = max(0, -6 - a * bx)
    x1 = min(bx, bx + 7 - a * bx)
    y0, y1 = {-1: (by - 8, by), 0: (0, by), 1: (0, 8)}[b]
    return x0, x1, y0, y1


def exchange_kernel(with_target, bx, by, *refs):
    if with_target:
        packet, target, packets, wide, send_sem, recv_sem = refs
    else:
        packet, packets, send_sem, recv_sem = refs
    s, q = lax.axis_index("cells"), lax.axis_index("grp")
    barrier = pltpu.get_barrier_semaphore()
    total = jnp.int32(0)
    for a, b in NEIGHBOURS:
        there = exists(a, b)
        total = total + there.astype(jnp.int32)

        @pl.when(there)
        def _(a=a, b=b):
            pl.semaphore_signal(barrier, inc=1, device_id=(s + a, q + b), device_id_type=MESH)

    pl.semaphore_wait(barrier, total)

    def copies(a, b):
        back = slot_of(-a, -b)
        out = [
            pltpu.make_async_remote_copy(
                src_ref=packet,
                dst_ref=packets.at[back],
                send_sem=send_sem.at[0, slot_of(a, b)],
                recv_sem=recv_sem.at[0, back],
                device_id=(s + a, q + b),
                device_id_type=MESH,
            )
        ]
        if with_target:
            x0, x1, y0, y1 = target_piece(-a, -b, bx, by)
            X = 6 - a * bx + x0
            Y = 8 - b * by + y0
            out.append(
                pltpu.make_async_remote_copy(
                    src_ref=target.at[x0:x1, y0:y1],
                    dst_ref=wide.at[X : X + x1 - x0, Y : Y + y1 - y0],
                    send_sem=send_sem.at[1, slot_of(a, b)],
                    recv_sem=recv_sem.at[1, back],
                    device_id=(s + a, q + b),
                    device_id_type=MESH,
                )
            )
        return out

    def arrivals(a, b):
        mine = slot_of(a, b)
        out = [
            pltpu.make_async_remote_copy(
                src_ref=packet,
                dst_ref=packets.at[mine],
                send_sem=send_sem.at[0, mine],
                recv_sem=recv_sem.at[0, mine],
                device_id=(s + a, q + b),
                device_id_type=MESH,
            )
        ]
        if with_target:
            x0, x1, y0, y1 = target_piece(a, b, bx, by)
            X = 6 + a * bx + x0
            Y = 8 + b * by + y0
            out.append(
                pltpu.make_async_remote_copy(
                    src_ref=target.at[x0:x1, y0:y1],
                    dst_ref=wide.at[X : X + x1 - x0, Y : Y + y1 - y0],
                    send_sem=send_sem.at[1, mine],
                    recv_sem=recv_sem.at[1, mine],
                    device_id=(s + a, q + b),
                    device_id_type=MESH,
                )
            )
        return out

    for a, b in NEIGHBOURS:

        @pl.when(exists(a, b))
        def _(a=a, b=b):
            for c in copies(a, b):
                c.start()

    for a, b in NEIGHBOURS:

        @pl.when(exists(a, b))
        def _(a=a, b=b):
            for c in arrivals(a, b):
                c.wait_recv()
            for c in copies(a, b):
                c.wait_send()


def exchange(packet, target, bx, by, gz, cid):
    with_target = target is not None
    out_shape = [jax.ShapeDtypeStruct((SLOTS,) + packet.shape, F32)]
    operands = [packet]
    if with_target:
        out_shape.append(jax.ShapeDtypeStruct((bx + 13, by + 16, gz), F32))
        operands.append(target)
    return pl.pallas_call(
        functools.partial(exchange_kernel, with_target, bx, by),
        out_shape=out_shape,
        in_specs=[ANY] * len(operands),
        out_specs=[ANY] * len(out_shape),
        scratch_shapes=[
            pltpu.SemaphoreType.DMA((2, SLOTS)),
            pltpu.SemaphoreType.DMA((2, SLOTS)),
        ],
        compiler_params=pltpu.CompilerParams(collective_id=cid, has_side_effects=True),
        name="exchange%d" % cid,
    )(*operands)


def split2(x):
    hi = x.astype(BF16)
    return hi, (x - hi.astype(F32)).astype(BF16)


def split3(x):
    hi = x.astype(BF16)
    rest = x - hi.astype(F32)
    mid = rest.astype(BF16)
    return hi, mid, (rest - mid.astype(F32)).astype(BF16)


def dot_nn(x, y):
    return lax.dot_general(x, y, (((1,), (0,)), ((), ())), preferred_element_type=F32)


def dot_nt(x, y):
    return lax.dot_general(x, y, (((1,), (1,)), ((), ())), preferred_element_type=F32)


def iota_f(shape, dim):
    return lax.broadcasted_iota(jnp.int32, shape, dim).astype(F32)


def tap_of(t):
    u = jnp.abs(t)
    return jnp.where(
        u == 0.0, TAPS[2], jnp.where(u == 1.0, TAPS[1], jnp.where(u == 2.0, TAPS[0], 0.0))
    )


def band(gz, radius, taps):
    i = lax.broadcasted_iota(jnp.int32, (gz, gz), 0)
    j = lax.broadcasted_iota(jnp.int32, (gz, gz), 1)
    t = (i - j).astype(F32)
    if taps:
        return tap_of(t).astype(BF16)
    return jnp.where(jnp.abs(t) <= radius, 1.0, 0.0).astype(BF16)


def step_kernel(first, last, bx, by, gz, n_x, n_y, *refs):
    if first:
        (counts, table, packets, own_packet, velocity, moved, wide, target,
         vel_out, moved_out, next_packet, pot, inv_ref, tgt_ref,
         pk, ch, sw, pos, feat, cols, acc, dens, wm) = refs
    else:
        (counts, table, packets, own_packet, velocity, moved, inv_ref, tgt_ref,
         vel_out, moved_out, pot,
         pk, ch, sw, pos, feat, cols, acc, dens) = refs
    atoms = own_packet.shape[1]
    s, q = lax.axis_index("cells"), lax.axis_index("grp")
    rx, ry = bx + 5, by + 8
    lane = lax.broadcasted_iota(jnp.int32, (8, atoms), 1)

    def count_of(a, b):
        slot = slot_of(a, b)
        return jnp.where(exists(a, b), counts[slot].astype(jnp.int32), 0)

    live_of = {}
    for a in range(-RX, RX + 1):
        for b in range(-RY, RY + 1):
            slot = slot_of(a, b)
            n = count_of(a, b)
            live_of[(a, b)] = n
            if slot == OWN:
                block = own_packet[...]
            else:
                block = packets[slot]
            block = jnp.where(lane < n, block, 0.0)
            pk[slot] = block
            kind = block[6:7]
            amp = jnp.zeros_like(kind)
            wid = jnp.zeros_like(kind)
            for t in range(table.shape[1]):
                amp = jnp.where(kind == float(t), table[0, t], amp)
                wid = jnp.where(kind == float(t), table[1, t], wid)
            charge = jnp.where(lane[0:1] < n, amp, 0.0)
            square = wid * wid
            px = block[0:1] + block[3:4] + float(a * bx)
            py = block[1:2] + block[4:5] + float(b * by)
            pz = block[2:3] + block[5:6]
            ch[slot] = charge
            pos[slot] = jnp.concatenate([px, py, pz, square, px, px, px, px], 0)
            if abs(a) <= 1:
                four = jnp.concatenate([charge, charge * px, charge * py, charge * pz], 0)
                h, m, l = split3(four)
                feat[slot] = jnp.concatenate(
                    [h.astype(F32), m.astype(F32), l.astype(F32), jnp.zeros_like(four)], 0
                )

    own_t = jnp.transpose(pos[OWN])
    for k in range(4):
        cols[k] = jnp.broadcast_to(own_t[:, k : k + 1], (atoms, 128))
    acc[...] = jnp.zeros_like(acc)
    half = atoms // 2
    own_live = live_of[(0, 0)]
    scale = -0.5 * math.log2(math.e)

    def pairs(start):
        xi = cols[0, start : start + half]
        rows = pl.ds(start, half)

        def per_slot(slot, carry):
            a = slot // NB - RX
            b = slot % NB - RY
            n = jnp.where(exists(a, b), counts[slot].astype(jnp.int32), 0)

            def per_block(block, inner):
                at = pl.ds(pl.multiple_of(block * 128, 128), 128)
                other = pos[slot, :, at]
                dx = cols[0, rows] - other[0:1]
                dy = cols[1, rows] - other[1:2]
                dz = cols[2, rows] - other[2:3]
                d2 = dx * dx + dy * dy + dz * dz
                inverse = 1.0 / (cols[3, rows] + other[3:4])
                value = jnp.exp2(d2 * inverse * scale) * inverse
                hi, lo = split2(value)
                f = feat[slot, :, at].astype(BF16)
                acc[rows] += dot_nt(
                    jnp.concatenate([hi, lo], 1), jnp.concatenate([f, f], 1)
                )
                return inner

            return lax.fori_loop(0, (n + 127) // 128, per_block, carry)

        lax.fori_loop(NB * (RX - 1), NB * (RX + 2), per_slot, 0)

    pairs(0)

    @pl.when(own_live > half)
    def _():
        pairs(half)

    dens[...] = jnp.zeros_like(dens)
    iz = iota_f((gz, half), 0)
    for a in range(-RX, RX + 1):
        p0 = max(0, a * bx)
        p1 = min(rx, a * bx + bx + 5)
        for b in range(-RY, RY + 1):
            r0, r1 = {-1: (0, 8), 0: (0, ry), 1: (by, ry)}[b]
            slot = slot_of(a, b)
            n = live_of[(a, b)]
            for start in (0, half):

                @pl.when(n > start)
                def _(a=a, b=b, slot=slot, start=start, p0=p0, p1=p1, r0=r0, r1=r1):
                    block = pk[slot, :, start : start + half]
                    charge = ch[slot, :, start : start + half]
                    ax, ay, az = block[0:1], block[1:2], block[2:3]
                    fx, fy, fz = block[3:4], block[4:5], block[5:6]
                    ax = ax + float(a * bx)
                    ay = ay + float(b * by)
                    in_x = ax + 1.0 + (s * bx).astype(F32) < float(n_x)
                    in_y = ay + 1.0 + (q * by).astype(F32) < float(n_y)
                    ux = jnp.where(in_x, fx, 0.0)
                    uy = jnp.where(in_y, fy, 0.0)
                    tx = iota_f((p1 - p0, half), 0) + float(p0 - 2) - ax
                    wx = tap_of(tx) * (1.0 - fx) + tap_of(tx - 1.0) * ux
                    ty = iota_f((r1 - r0, half), 0) + float(r0 - 2) - ay
                    wy = tap_of(ty) * (1.0 - fy) + tap_of(ty - 1.0) * uy
                    plane = jnp.concatenate([wy * wx[p : p + 1] for p in range(p1 - p0)], 0)
                    ph, plo = split2(plane)
                    lower_h, lower_l = split2(charge * (1.0 - fz))
                    upper_h, upper_l = split2(charge * fz)
                    at_low = iz == az
                    at_up = iz == az + 1.0
                    zh = jnp.where(
                        at_low, lower_h.astype(F32), jnp.where(at_up, upper_h.astype(F32), 0.0)
                    ).astype(BF16)
                    zl = jnp.where(
                        at_low, lower_l.astype(F32), jnp.where(at_up, upper_l.astype(F32), 0.0)
                    ).astype(BF16)
                    both = dot_nt(jnp.concatenate([ph, plo], 0), zh)
                    size = plane.shape[0]
                    summed = both[:size] + both[size:] + dot_nt(ph, zl)
                    dens[p0:p1, r0:r1] += summed.reshape(p1 - p0, r1 - r0, gz)

    blur_z = band(gz, 2, True)

    def z_blur(x):
        h, l = split2(x)
        size = x.shape[0]
        both = dot_nn(jnp.concatenate([h, l], 0), blur_z)
        return both[:size] + both[size:]

    gx = lax.broadcasted_iota(jnp.int32, (rx, ry, gz), 0) - 2 + s * bx
    gy = lax.broadcasted_iota(jnp.int32, (rx, ry, gz), 1) - 2 + q * by
    inside = (gx >= 0) & (gx < n_x) & (gy >= 0) & (gy < n_y)

    if first:
        wxp, wyp = bx + 13, by + 16
        tx = lax.broadcasted_iota(jnp.int32, (wxp, wyp, gz), 0) - 6 + s * bx
        ty = lax.broadcasted_iota(jnp.int32, (wxp, wyp, gz), 1) - 8 + q * by
        valid = (tx >= 0) & (tx < n_x) & (ty >= 0) & (ty < n_y)
        wm[...] = jnp.where(valid, wide[...], 0.0)
        wm[6 : 6 + bx, 8 : 8 + by] = target[...]
        t = wm[...]

        box_z = band(gz, 4, False)

        def boxed(v):
            two = v[:-1] + v[1:]
            four = two[:-2] + two[2:]
            eight = four[:-4] + four[4:]
            v = eight[:rx] + v[8 : 8 + rx]
            size = wyp
            two = v + pltpu.roll(v, size - 1, 1)
            four = two + pltpu.roll(two, size - 2, 1)
            eight = four + pltpu.roll(four, size - 4, 1)
            nine = eight + pltpu.roll(v, size - 8, 1)
            v = pltpu.roll(nine, size - 2, 1)[:, :ry]
            v = v.reshape(rx * ry, gz)
            h, m, l = split3(v)
            size = v.shape[0]
            out = dot_nn(jnp.concatenate([h, m, l], 0), box_z)
            out = out[:size] + out[size : 2 * size] + out[2 * size :]
            return out.reshape(rx, ry, gz) * (1.0 / 729.0)

        mean_one = boxed(t)
        mean_two = boxed(t * t)
        inverse_scale = lax.rsqrt(mean_two - mean_one * mean_one + EPSILON)
        inverse_scale = jnp.where(inside, inverse_scale, 0.0)
        near = pltpu.roll(t[4 : 4 + rx], wyp - 6, 1)[:, :ry]
        inv_ref[...] = inverse_scale
        tgt_ref[...] = near
    else:
        inverse_scale = inv_ref[...]
        near = tgt_ref[...]

    blurred = z_blur(dens[...].reshape(rx * ry, gz)).reshape(rx, ry, gz)
    residual = jnp.where(inside, (blurred - near) * inverse_scale, 0.0)
    along = TAPS[0] * (residual[0 : bx + 1] + residual[4 : bx + 5])
    along = along + TAPS[1] * (residual[1 : bx + 2] + residual[3 : bx + 4])
    along = along + TAPS[2] * residual[2 : bx + 3]
    down = TAPS[0] * along
    for k in range(1, 5):
        down = down + TAPS[k] * pltpu.roll(along, ry - k, 1)
    potential = z_blur(down.reshape((bx + 1) * ry, gz)).reshape(bx + 1, ry, gz)
    pot[...] = potential[:bx, :by]
    px = lax.broadcasted_iota(jnp.int32, (bx + 1, ry, gz), 0) + s * bx
    py = lax.broadcasted_iota(jnp.int32, (bx + 1, ry, gz), 1) + q * by
    py_local = lax.broadcasted_iota(jnp.int32, (bx + 1, ry, gz), 1)
    field = jnp.where((px < n_x) & (py < n_y) & (py_local <= by), potential, 0.0)

    own = pk[OWN]
    charge = ch[OWN]
    ax, ay, az = own[0:1], own[1:2], own[2:3]
    fx, fy, fz = own[3:4], own[4:5], own[5:6]
    iz = iota_f((gz, atoms), 0)
    at_low = iz == az
    at_up = iz == az + 1.0
    zh, zl = split2(jnp.where(at_low, charge * (1.0 - fz), jnp.where(at_up, charge * fz, 0.0)))
    gh, gl = split2(jnp.where(at_low, -charge, jnp.where(at_up, charge, 0.0)))
    size = (bx + 1) * ry
    fh, fl = split2(field.reshape(size, gz))
    fboth = jnp.concatenate([fh, fl], 0)

    def sampled(h, l):
        both = dot_nn(fboth, h)
        return both[:size] + both[size:] + dot_nn(fh, l)

    value = sampled(zh, zl)
    slope = sampled(gh, gl)
    iy = iota_f((ry, atoms), 0)
    low_y = jnp.where(iy == ay, 1.0, 0.0)
    up_y = jnp.where(iy == ay + 1.0, 1.0, 0.0)
    wy = low_y * (1.0 - fy) + up_y * fy
    sy = up_y - low_y
    grad_x = jnp.zeros((1, atoms), F32)
    grad_y = jnp.zeros((1, atoms), F32)
    grad_z = jnp.zeros((1, atoms), F32)
    for p in range(bx + 1):
        low_x = jnp.where(ax == float(p), 1.0, 0.0)
        up_x = jnp.where(ax + 1.0 == float(p), 1.0, 0.0)
        wx = low_x * (1.0 - fx) + up_x * fx
        sx = up_x - low_x
        v = value[p * ry : (p + 1) * ry]
        g = slope[p * ry : (p + 1) * ry]
        grad_x = grad_x + sx * jnp.sum(wy * v, 0, keepdims=True)
        grad_y = grad_y + wx * jnp.sum(sy * v, 0, keepdims=True)
        grad_z = grad_z + wx * jnp.sum(wy * g, 0, keepdims=True)
    gradient = jnp.concatenate([grad_x, grad_y, grad_z], 0)

    sums = jnp.transpose(acc[...])
    sums = sums[0:4] + sums[4:8] + sums[8:12]
    here = pos[OWN][0:3]
    pair = charge * (here * sums[0:1] - sums[1:4])
    mass = jnp.ones_like(charge)
    for t in range(table.shape[1]):
        mass = jnp.where(own[6:7] == float(t), table[2, t], mass)
    new_velocity = velocity[...] + TIME_STEP * (pair - gradient) / mass
    new_moved = moved[...] + TIME_STEP * new_velocity
    if last:
        live = lane[0:3] < own_live
        vel_out[...] = jnp.where(live, new_velocity, 0.0)
        moved_out[...] = jnp.where(live, new_moved, 0.0)
    else:
        vel_out[...] = new_velocity
        moved_out[...] = new_moved
        next_packet[...] = jnp.concatenate(
            [own[0:3], own[3:6] + TIME_STEP * new_velocity, own[6:8]], 0
        )


def step_call(first, last, sizes, operands, out_shape):
    bx, by, gz, n_x, n_y, atoms = sizes
    scratch = [
        pltpu.VMEM((SLOTS, 8, atoms), F32),
        pltpu.VMEM((SLOTS, 1, atoms), F32),
        pltpu.VMEM((SLOTS, 1, atoms), F32),
        pltpu.VMEM((SLOTS, 8, atoms), F32),
        pltpu.VMEM((SLOTS, 16, atoms), F32),
        pltpu.VMEM((4, atoms, 128), F32),
        pltpu.VMEM((atoms, 16), F32),
        pltpu.VMEM((bx + 5, by + 8, gz), F32),
    ]
    if first:
        scratch.append(pltpu.VMEM((bx + 13, by + 16, gz), F32))
    return pl.pallas_call(
        functools.partial(step_kernel, first, last, bx, by, gz, n_x, n_y),
        out_shape=out_shape,
        in_specs=[SMEM, SMEM] + [VMEM] * (len(operands) - 2),
        out_specs=[VMEM] * len(out_shape),
        scratch_shapes=scratch,
        name="first_step" if first else "last_step",
    )(*operands)


def per_device(fraction, velocity, anchor, atom_types, counts, type_table, target):
    atoms = fraction.shape[3]
    bx, by, gz = target.shape
    n_x = bx * lax.axis_size("cells")
    n_y = by * lax.axis_size("grp")
    fraction = fraction.reshape(3, atoms)
    velocity = velocity.reshape(3, atoms)
    packet = jnp.concatenate(
        [
            anchor.reshape(3, atoms).astype(F32),
            fraction,
            atom_types.reshape(1, atoms).astype(F32),
            jnp.broadcast_to(counts.astype(F32), (1, atoms)),
        ],
        0,
    )
    packets, wide = exchange(packet, target, bx, by, gz, 0)
    live_counts = packets[:, 7, 0].at[OWN].set(counts[0, 0].astype(F32))
    sizes = (bx, by, gz, n_x, n_y, atoms)
    row = jax.ShapeDtypeStruct((3, atoms), F32)
    field = jax.ShapeDtypeStruct((bx, by, gz), F32)
    region = jax.ShapeDtypeStruct((bx + 5, by + 8, gz), F32)
    moved = jnp.zeros((3, atoms), F32)
    velocity, moved, next_packet, _, inverse, near = step_call(
        True, False, sizes,
        (live_counts, type_table, packets, packet, velocity, moved, wide, target),
        [row, row, jax.ShapeDtypeStruct((8, atoms), F32), field, region, region],
    )
    (later,) = exchange(next_packet, None, bx, by, gz, 1)
    velocity, moved, potential = step_call(
        False, True, sizes,
        (live_counts, type_table, later, next_packet, velocity, moved, inverse, near),
        [row, row, field],
    )
    return (
        velocity.reshape(3, 1, 1, atoms),
        moved.reshape(3, 1, 1, atoms),
        potential,
    )


def solution(mesh):
    placed = (
        P(None, "cells", "grp", None),
        P(None, "cells", "grp", None),
        P(None, "cells", "grp", None),
        P("cells", "grp", None),
        P("cells", "grp"),
        P(),
        P("cells", "grp", None),
    )
    return jax.shard_map(
        per_device,
        mesh=mesh,
        in_specs=placed,
        out_specs=(
            P(None, "cells", "grp", None),
            P(None, "cells", "grp", None),
            P("cells", "grp", None),
        ),
        check_vma=False,
    )
```

```python
import functools
import math

import jax
import jax.numpy as jnp
from jax import lax
from jax.experimental import pallas as pl
from jax.experimental.pallas import tpu as pltpu
from jax.sharding import PartitionSpec as P

EPSILON = 1e-06
TIME_STEP = 0.5
TAPS = (1.0 / 16.0, 4.0 / 16.0, 6.0 / 16.0, 4.0 / 16.0, 1.0 / 16.0)
F32 = jnp.float32
BF16 = jnp.bfloat16
RX, RY = 2, 1
NB = 2 * RY + 1
SLOTS = (2 * RX + 1) * NB
OWN = RX * NB + RY
MESH = pl.DeviceIdType.MESH
VMEM = pl.BlockSpec(memory_space=pltpu.VMEM)
SMEM = pl.BlockSpec(memory_space=pltpu.SMEM)
ANY = pl.BlockSpec(memory_space=pl.ANY)
NEIGHBOURS = tuple(
    (a, b) for a in range(-RX, RX + 1) for b in range(-RY, RY + 1) if (a, b) != (0, 0)
)


def slot_of(a, b):
    return (a + RX) * NB + (b + RY)


def exists(a, b):
    s = lax.axis_index("cells") + a
    q = lax.axis_index("grp") + b
    ns, nq = lax.axis_size("cells"), lax.axis_size("grp")
    return (s >= 0) & (s < ns) & (q >= 0) & (q < nq)


def target_piece(a, b, bx, by):
    x0 = max(0, -6 - a * bx)
    x1 = min(bx, bx + 7 - a * bx)
    y0, y1 = {-1: (by - 8, by), 0: (0, by), 1: (0, 8)}[b]
    return x0, x1, y0, y1


def exchange_kernel(with_target, bx, by, *refs):
    if with_target:
        packet, target, count, packets, wide, counts, send_sem, recv_sem = refs
    else:
        packet, packets, send_sem, recv_sem = refs
    s, q = lax.axis_index("cells"), lax.axis_index("grp")
    barrier = pltpu.get_barrier_semaphore()
    total = jnp.int32(0)
    for a, b in NEIGHBOURS:
        there = exists(a, b)
        total = total + there.astype(jnp.int32)

        @pl.when(there)
        def _(a=a, b=b):
            pl.semaphore_signal(barrier, inc=1, device_id=(s + a, q + b), device_id_type=MESH)

    pl.semaphore_wait(barrier, total)

    def copies(a, b):
        back = slot_of(-a, -b)
        out = [
            pltpu.make_async_remote_copy(
                src_ref=packet,
                dst_ref=packets.at[back],
                send_sem=send_sem.at[0, slot_of(a, b)],
                recv_sem=recv_sem.at[0, back],
                device_id=(s + a, q + b),
                device_id_type=MESH,
            )
        ]
        if with_target:
            x0, x1, y0, y1 = target_piece(-a, -b, bx, by)
            X = 6 - a * bx + x0
            Y = 8 - b * by + y0
            out.append(
                pltpu.make_async_remote_copy(
                    src_ref=target.at[x0:x1, y0:y1],
                    dst_ref=wide.at[X : X + x1 - x0, Y : Y + y1 - y0],
                    send_sem=send_sem.at[1, slot_of(a, b)],
                    recv_sem=recv_sem.at[1, back],
                    device_id=(s + a, q + b),
                    device_id_type=MESH,
                )
            )
            out.append(
                pltpu.make_async_remote_copy(
                    src_ref=count,
                    dst_ref=counts.at[back],
                    send_sem=send_sem.at[2, slot_of(a, b)],
                    recv_sem=recv_sem.at[2, back],
                    device_id=(s + a, q + b),
                    device_id_type=MESH,
                )
            )
        return out

    def arrivals(a, b):
        mine = slot_of(a, b)
        out = [
            pltpu.make_async_remote_copy(
                src_ref=packet,
                dst_ref=packets.at[mine],
                send_sem=send_sem.at[0, mine],
                recv_sem=recv_sem.at[0, mine],
                device_id=(s + a, q + b),
                device_id_type=MESH,
            )
        ]
        if with_target:
            x0, x1, y0, y1 = target_piece(a, b, bx, by)
            X = 6 + a * bx + x0
            Y = 8 + b * by + y0
            out.append(
                pltpu.make_async_remote_copy(
                    src_ref=target.at[x0:x1, y0:y1],
                    dst_ref=wide.at[X : X + x1 - x0, Y : Y + y1 - y0],
                    send_sem=send_sem.at[1, mine],
                    recv_sem=recv_sem.at[1, mine],
                    device_id=(s + a, q + b),
                    device_id_type=MESH,
                )
            )
            out.append(
                pltpu.make_async_remote_copy(
                    src_ref=count,
                    dst_ref=counts.at[mine],
                    send_sem=send_sem.at[2, mine],
                    recv_sem=recv_sem.at[2, mine],
                    device_id=(s + a, q + b),
                    device_id_type=MESH,
                )
            )
        return out

    for a, b in NEIGHBOURS:

        @pl.when(exists(a, b))
        def _(a=a, b=b):
            for c in copies(a, b):
                c.start()

    for a, b in NEIGHBOURS:

        @pl.when(exists(a, b))
        def _(a=a, b=b):
            for c in arrivals(a, b):
                c.wait_recv()
            for c in copies(a, b):
                c.wait_send()


def exchange(packet, target, count, bx, by, gz, cid):
    with_target = target is not None
    out_shape = [jax.ShapeDtypeStruct((SLOTS,) + packet.shape, F32)]
    operands = [packet]
    if with_target:
        out_shape.append(jax.ShapeDtypeStruct((bx + 13, by + 16, gz), F32))
        out_shape.append(jax.ShapeDtypeStruct((SLOTS,) + count.shape, F32))
        operands.extend([target, count])
    return pl.pallas_call(
        functools.partial(exchange_kernel, with_target, bx, by),
        out_shape=out_shape,
        in_specs=[ANY] * len(operands),
        out_specs=[ANY] * len(out_shape),
        scratch_shapes=[
            pltpu.SemaphoreType.DMA((3, SLOTS)),
            pltpu.SemaphoreType.DMA((3, SLOTS)),
        ],
        compiler_params=pltpu.CompilerParams(collective_id=cid, has_side_effects=True),
        name="exchange%d" % cid,
    )(*operands)


def split2(x):
    hi = x.astype(BF16)
    return hi, (x - hi.astype(F32)).astype(BF16)


def split3(x):
    hi = x.astype(BF16)
    rest = x - hi.astype(F32)
    mid = rest.astype(BF16)
    return hi, mid, (rest - mid.astype(F32)).astype(BF16)


def dot_nn(x, y):
    return lax.dot_general(x, y, (((1,), (0,)), ((), ())), preferred_element_type=F32)


def dot_nt(x, y):
    return lax.dot_general(x, y, (((1,), (1,)), ((), ())), preferred_element_type=F32)


def iota_f(shape, dim):
    return lax.broadcasted_iota(jnp.int32, shape, dim).astype(F32)


def tap_of(t):
    u = jnp.abs(t)
    return jnp.where(
        u == 0.0, TAPS[2], jnp.where(u == 1.0, TAPS[1], jnp.where(u == 2.0, TAPS[0], 0.0))
    )


def z_weights(iz, az, lower, upper):
    low_h, low_l = split2(lower)
    up_h, up_l = split2(upper)
    at_low = iz == az.astype(BF16)
    at_up = iz == (az + 1.0).astype(BF16)
    zero = jnp.zeros((), BF16)
    high = jnp.where(at_low, low_h, jnp.where(at_up, up_h, zero))
    return high, jnp.where(at_low, low_l, jnp.where(at_up, up_l, zero))


def band(gz, radius, taps):
    i = lax.broadcasted_iota(jnp.int32, (gz, gz), 0)
    j = lax.broadcasted_iota(jnp.int32, (gz, gz), 1)
    t = (i - j).astype(F32)
    if taps:
        return tap_of(t).astype(BF16)
    return jnp.where(jnp.abs(t) <= radius, 1.0, 0.0).astype(BF16)


def pack_kernel(fraction, anchor, kinds, counts, table, packet, mass, count):
    atoms = packet.shape[1]
    n = counts[0, 0]
    kind = kinds[0]
    lane = lax.broadcasted_iota(jnp.int32, (1, atoms), 1)
    rows = []
    for r in range(3):
        row = jnp.zeros((1, atoms), F32)
        for t in range(table.shape[1]):
            row = jnp.where(kind == t, table[r, t], row)
        rows.append(row)
    packet[0:3] = anchor[:, 0, 0, :].astype(F32)
    packet[3:6] = fraction[:, 0, 0, :]
    packet[6:7] = jnp.where(lane < n, rows[0], 0.0)
    packet[7:8] = rows[1] * rows[1]
    mass[...] = rows[2]
    count[...] = jnp.full(count.shape, n.astype(F32))


SPREAD = -2.0 / math.log2(math.e)


def step_kernel(first, last, bx, by, gz, n_x, n_y, *refs):
    if first:
        (own_count, counts, packets, own_packet, mass, velocity, wide, target,
         vel_out, moved_out, next_packet, pot, inv_ref, tgt_ref,
         pk, pos, feat, cols, acc, dens, wm) = refs
    else:
        (own_count, counts, packets, own_packet, mass, velocity, moved, inv_ref, tgt_ref,
         vel_out, moved_out, pot,
         pk, pos, feat, cols, acc, dens) = refs
    atoms = own_packet.shape[1]
    s, q = lax.axis_index("cells"), lax.axis_index("grp")
    rx, ry = bx + 5, by + 8
    own_live = own_count[0, 0]

    def live_in(slot, a, b):
        n = jnp.where(exists(a, b), counts[slot, 0, 0].astype(jnp.int32), 0)
        return jnp.where(slot == OWN, own_live, n)

    row = lax.broadcasted_iota(jnp.int32, (8, atoms), 0)
    for a in range(-RX, RX + 1):
        for b in range(-RY, RY + 1):
            slot = slot_of(a, b)
            if slot == OWN:
                block = own_packet[...]
            else:
                block = jnp.where(exists(a, b), packets[slot], 0.0)
            pk[slot] = block
            if abs(a) <= 1:
                base = jnp.where(row == 0, float(a * bx), jnp.where(row == 1, float(b * by), 0.0))
                place = jnp.where(
                    row < 3, block + pltpu.roll(block, 5, 0) + base, pltpu.roll(block, 4, 0) * SPREAD
                )
                pos[slot] = place
                four = jnp.where(row < 3, place, jnp.where(row == 3, 1.0, 0.0)) * block[6:7]
                h, m, l = split3(four)
                feat[slot] = jnp.concatenate([h.astype(F32), m.astype(F32), l.astype(F32)], 0)

    own_t = jnp.transpose(pos[OWN])
    for k in range(4):
        cols[k] = jnp.broadcast_to(own_t[:, k : k + 1], (atoms, 128))
    acc[...] = jnp.zeros_like(acc)
    half = atoms // 2

    def pairs(height):
        rows = pl.ds(0, height)

        def add(tile):
            both, f = tile
            acc[rows] += dot_nt(both, f)

        def per_slot(slot, carry):
            n = live_in(slot, slot // NB - RX, slot % NB - RY)

            def per_block(block, carry):
                add(carry)
                at = pl.ds(pl.multiple_of(block * 128, 128), 128)
                other = pos[slot, :, at]
                dx = cols[0, rows] - other[0:1]
                dy = cols[1, rows] - other[1:2]
                dz = cols[2, rows] - other[2:3]
                d2 = dx * dx + dy * dy + dz * dz
                inverse = 1.0 / (cols[3, rows] + other[3:4])
                value = jnp.exp2(d2 * inverse) * inverse
                hi, lo = split2(value)
                f = feat[slot, :, at].astype(BF16)
                return jnp.concatenate([hi, lo], 1), jnp.concatenate([f, f], 1)

            return lax.fori_loop(0, (n + 127) // 128, per_block, carry)

        empty = (jnp.zeros((height, 256), BF16), jnp.zeros((24, 256), BF16))
        add(lax.fori_loop(NB * (RX - 1), NB * (RX + 2), per_slot, empty))

    @pl.when(own_live <= half)
    def _():
        pairs(half)

    @pl.when(own_live > half)
    def _():
        pairs(atoms)

    iz = iota_f((gz, half), 0).astype(BF16)

    def spread(a, b, start):
        p0 = max(0, a * bx)
        p1 = min(rx, a * bx + bx + 5)
        r0, r1 = {-1: (0, 8), 0: (0, ry), 1: (by, ry)}[b]
        block = pk[slot_of(a, b), :, start : start + half]
        charge = block[6:7]
        ax, ay, az = block[0:1], block[1:2], block[2:3]
        fx, fy, fz = block[3:4], block[4:5], block[5:6]
        ax = ax + float(a * bx)
        ay = ay + float(b * by)
        in_x = ax + 1.0 + (s * bx).astype(F32) < float(n_x)
        in_y = ay + 1.0 + (q * by).astype(F32) < float(n_y)
        ux = jnp.where(in_x, fx, 0.0)
        uy = jnp.where(in_y, fy, 0.0)
        tx = iota_f((p1 - p0, half), 0) + float(p0 - 2) - ax
        wx = tap_of(tx) * (1.0 - fx) + tap_of(tx - 1.0) * ux
        ty = iota_f((r1 - r0, half), 0) + float(r0 - 2) - ay
        wy = tap_of(ty) * (1.0 - fy) + tap_of(ty - 1.0) * uy
        plane = jnp.concatenate([wy * wx[p : p + 1] for p in range(p1 - p0)], 0)
        ph, plo = split2(plane)
        zh, zl = z_weights(iz, az, charge * (1.0 - fz), charge * fz)
        both = dot_nt(jnp.concatenate([ph, plo], 0), zh)
        size = plane.shape[0]
        summed = both[:size] + both[size:] + dot_nt(ph, zl)
        dens[p0:p1, r0:r1] += summed.reshape(p1 - p0, r1 - r0, gz)

    dens[...] = jnp.zeros_like(dens)
    cells = [(0, 0)] + list(NEIGHBOURS)
    for a, b in cells:
        spread(a, b, 0)
    for a, b in cells:

        @pl.when(live_in(slot_of(a, b), a, b) > half)
        def _(a=a, b=b):
            spread(a, b, half)

    blur_z = band(gz, 2, True)

    def z_blur(x):
        h, l = split2(x)
        size = x.shape[0]
        both = dot_nn(jnp.concatenate([h, l], 0), blur_z)
        return both[:size] + both[size:]

    gx = lax.broadcasted_iota(jnp.int32, (rx, ry, gz), 0) - 2 + s * bx
    gy = lax.broadcasted_iota(jnp.int32, (rx, ry, gz), 1) - 2 + q * by
    inside = (gx >= 0) & (gx < n_x) & (gy >= 0) & (gy < n_y)

    if first:
        wxp, wyp = bx + 13, by + 16
        tx = lax.broadcasted_iota(jnp.int32, (wxp, wyp, gz), 0) - 6 + s * bx
        ty = lax.broadcasted_iota(jnp.int32, (wxp, wyp, gz), 1) - 8 + q * by
        valid = (tx >= 0) & (tx < n_x) & (ty >= 0) & (ty < n_y)
        wm[...] = jnp.where(valid, wide[...], 0.0)
        wm[6 : 6 + bx, 8 : 8 + by] = target[...]
        t = wm[...]

        box_z = band(gz, 4, False)

        def boxed(v):
            two = v[:-1] + v[1:]
            four = two[:-2] + two[2:]
            eight = four[:-4] + four[4:]
            v = eight[:rx] + v[8 : 8 + rx]
            size = wyp
            two = v + pltpu.roll(v, size - 1, 1)
            four = two + pltpu.roll(two, size - 2, 1)
            eight = four + pltpu.roll(four, size - 4, 1)
            nine = eight + pltpu.roll(v, size - 8, 1)
            v = pltpu.roll(nine, size - 2, 1)[:, :ry]
            v = v.reshape(rx * ry, gz)
            h, m, l = split3(v)
            size = v.shape[0]
            out = dot_nn(jnp.concatenate([h, m, l], 0), box_z)
            out = out[:size] + out[size : 2 * size] + out[2 * size :]
            return out.reshape(rx, ry, gz) * (1.0 / 729.0)

        mean_one = boxed(t)
        mean_two = boxed(t * t)
        inverse_scale = lax.rsqrt(mean_two - mean_one * mean_one + EPSILON)
        inverse_scale = jnp.where(inside, inverse_scale, 0.0)
        near = pltpu.roll(t[4 : 4 + rx], wyp - 6, 1)[:, :ry]
        inv_ref[...] = inverse_scale
        tgt_ref[...] = near
    else:
        inverse_scale = inv_ref[...]
        near = tgt_ref[...]

    blurred = z_blur(dens[...].reshape(rx * ry, gz)).reshape(rx, ry, gz)
    residual = jnp.where(inside, (blurred - near) * inverse_scale, 0.0)
    along = TAPS[0] * (residual[0 : bx + 1] + residual[4 : bx + 5])
    along = along + TAPS[1] * (residual[1 : bx + 2] + residual[3 : bx + 4])
    along = along + TAPS[2] * residual[2 : bx + 3]
    down = TAPS[0] * along
    for k in range(1, 5):
        down = down + TAPS[k] * pltpu.roll(along, ry - k, 1)
    potential = z_blur(down.reshape((bx + 1) * ry, gz)).reshape(bx + 1, ry, gz)
    pot[...] = potential[:bx, :by]
    px = lax.broadcasted_iota(jnp.int32, (bx + 1, ry, gz), 0) + s * bx
    py = lax.broadcasted_iota(jnp.int32, (bx + 1, ry, gz), 1) + q * by
    py_local = lax.broadcasted_iota(jnp.int32, (bx + 1, ry, gz), 1)
    field = jnp.where((px < n_x) & (py < n_y) & (py_local <= by), potential, 0.0)

    own = pk[OWN]
    charge = own[6:7]
    ax, ay, az = own[0:1], own[1:2], own[2:3]
    fx, fy, fz = own[3:4], own[4:5], own[5:6]
    iz = iota_f((gz, atoms), 0).astype(BF16)
    zh, zl = z_weights(iz, az, charge * (1.0 - fz), charge * fz)
    gh, gl = z_weights(iz, az, -charge, charge)
    size = (bx + 1) * ry
    fh, fl = split2(field.reshape(size, gz))
    fboth = jnp.concatenate([fh, fl], 0)

    def sampled(h, l):
        both = dot_nn(fboth, h)
        return both[:size] + both[size:] + dot_nn(fh, l)

    value = sampled(zh, zl)
    slope = sampled(gh, gl)
    iy = iota_f((ry, atoms), 0)
    low_y = jnp.where(iy == ay, 1.0, 0.0)
    up_y = jnp.where(iy == ay + 1.0, 1.0, 0.0)
    wy = low_y * (1.0 - fy) + up_y * fy
    sy = up_y - low_y
    grad_x = jnp.zeros((1, atoms), F32)
    grad_y = jnp.zeros((1, atoms), F32)
    grad_z = jnp.zeros((1, atoms), F32)
    for p in range(bx + 1):
        low_x = jnp.where(ax == float(p), 1.0, 0.0)
        up_x = jnp.where(ax + 1.0 == float(p), 1.0, 0.0)
        wx = low_x * (1.0 - fx) + up_x * fx
        sx = up_x - low_x
        v = value[p * ry : (p + 1) * ry]
        g = slope[p * ry : (p + 1) * ry]
        grad_x = grad_x + sx * jnp.sum(wy * v, 0, keepdims=True)
        grad_y = grad_y + wx * jnp.sum(sy * v, 0, keepdims=True)
        grad_z = grad_z + wx * jnp.sum(wy * g, 0, keepdims=True)
    gradient = jnp.concatenate([grad_x, grad_y, grad_z], 0)

    sums = jnp.transpose(acc[...])
    sums = sums[0:8] + sums[8:16] + sums[16:24]
    here = pos[OWN][0:3]
    pair = (SPREAD * charge) * (here * sums[3:4] - sums[0:3])
    old_velocity = velocity[:, 0, 0, :] if first else velocity[...]
    new_velocity = old_velocity + TIME_STEP * (pair - gradient) / mass[...]
    new_moved = TIME_STEP * new_velocity
    if not first:
        new_moved = moved[...] + new_moved
    if last:
        live = lax.broadcasted_iota(jnp.int32, (3, atoms), 1) < own_live
        vel_out[:, 0, 0, :] = jnp.where(live, new_velocity, 0.0)
        moved_out[:, 0, 0, :] = jnp.where(live, new_moved, 0.0)
    else:
        vel_out[...] = new_velocity
        moved_out[...] = new_moved
        next_packet[...] = jnp.concatenate(
            [own[0:3], own[3:6] + TIME_STEP * new_velocity, own[6:8]], 0
        )


def step_call(first, last, sizes, operands, out_shape):
    bx, by, gz, n_x, n_y, atoms = sizes
    scratch = [
        pltpu.VMEM((SLOTS, 8, atoms), F32),
        pltpu.VMEM((SLOTS, 8, atoms), F32),
        pltpu.VMEM((SLOTS, 24, atoms), F32),
        pltpu.VMEM((4, atoms, 128), F32),
        pltpu.VMEM((atoms, 24), F32),
        pltpu.VMEM((bx + 5, by + 8, gz), F32),
    ]
    if first:
        scratch.append(pltpu.VMEM((bx + 13, by + 16, gz), F32))
    return pl.pallas_call(
        functools.partial(step_kernel, first, last, bx, by, gz, n_x, n_y),
        out_shape=out_shape,
        in_specs=[SMEM, SMEM] + [VMEM] * (len(operands) - 2),
        out_specs=[VMEM] * len(out_shape),
        scratch_shapes=scratch,
        name="first_step" if first else "last_step",
    )(*operands)


def per_device(fraction, velocity, anchor, atom_types, counts, type_table, target):
    atoms = fraction.shape[3]
    bx, by, gz = target.shape
    n_x = bx * lax.axis_size("cells")
    n_y = by * lax.axis_size("grp")
    packet, mass, count = pl.pallas_call(
        pack_kernel,
        out_shape=[
            jax.ShapeDtypeStruct((8, atoms), F32),
            jax.ShapeDtypeStruct((1, atoms), F32),
            jax.ShapeDtypeStruct((1, 128), F32),
        ],
        in_specs=[VMEM, VMEM, VMEM, SMEM, SMEM],
        out_specs=[VMEM] * 3,
        name="pack",
    )(fraction, anchor, atom_types, counts, type_table)
    packets, wide, near_counts = exchange(packet, target, count, bx, by, gz, 0)
    sizes = (bx, by, gz, n_x, n_y, atoms)
    row = jax.ShapeDtypeStruct((3, atoms), F32)
    final = jax.ShapeDtypeStruct(velocity.shape, F32)
    field = jax.ShapeDtypeStruct((bx, by, gz), F32)
    region = jax.ShapeDtypeStruct((bx + 5, by + 8, gz), F32)
    velocity, moved, next_packet, _, inverse, near = step_call(
        True, False, sizes,
        (counts, near_counts, packets, packet, mass, velocity, wide, target),
        [row, row, jax.ShapeDtypeStruct((8, atoms), F32), field, region, region],
    )
    (later,) = exchange(next_packet, None, None, bx, by, gz, 1)
    return tuple(
        step_call(
            False, True, sizes,
            (counts, near_counts, later, next_packet, mass, velocity, moved, inverse, near),
            [final, final, field],
        )
    )


def solution(mesh):
    placed = (
        P(None, "cells", "grp", None),
        P(None, "cells", "grp", None),
        P(None, "cells", "grp", None),
        P("cells", "grp", None),
        P("cells", "grp"),
        P(),
        P("cells", "grp", None),
    )
    return jax.shard_map(
        per_device,
        mesh=mesh,
        in_specs=placed,
        out_specs=(
            P(None, "cells", "grp", None),
            P(None, "cells", "grp", None),
            P("cells", "grp", None),
        ),
        check_vma=False,
    )
```

```python
import functools
import math

import jax
import jax.numpy as jnp
from jax import lax
from jax.experimental import pallas as pl
from jax.experimental.pallas import tpu as pltpu
from jax.sharding import PartitionSpec as P

EPSILON = 1e-06
TIME_STEP = 0.5
TAPS = (1.0 / 16.0, 4.0 / 16.0, 6.0 / 16.0, 4.0 / 16.0, 1.0 / 16.0)
F32 = jnp.float32
BF16 = jnp.bfloat16
RX, RY = 2, 1
NB = 2 * RY + 1
SLOTS = (2 * RX + 1) * NB
OWN = RX * NB + RY
MESH = pl.DeviceIdType.MESH
VMEM = pl.BlockSpec(memory_space=pltpu.VMEM)
SMEM = pl.BlockSpec(memory_space=pltpu.SMEM)
ANY = pl.BlockSpec(memory_space=pl.ANY)
NEIGHBOURS = tuple(
    (a, b) for a in range(-RX, RX + 1) for b in range(-RY, RY + 1) if (a, b) != (0, 0)
)


def slot_of(a, b):
    return (a + RX) * NB + (b + RY)


def exists(a, b):
    s = lax.axis_index("cells") + a
    q = lax.axis_index("grp") + b
    ns, nq = lax.axis_size("cells"), lax.axis_size("grp")
    return (s >= 0) & (s < ns) & (q >= 0) & (q < nq)


def target_piece(a, b, bx, by):
    x0 = max(0, -6 - a * bx)
    x1 = min(bx, bx + 7 - a * bx)
    y0, y1 = {-1: (by - 8, by), 0: (0, by), 1: (0, 8)}[b]
    return x0, x1, y0, y1


def exchange_kernel(with_target, bx, by, *refs):
    if with_target:
        packet, target, count, packets, wide, counts, send_sem, recv_sem = refs
    else:
        packet, packets, send_sem, recv_sem = refs
    s, q = lax.axis_index("cells"), lax.axis_index("grp")
    barrier = pltpu.get_barrier_semaphore()
    total = jnp.int32(0)
    for a, b in NEIGHBOURS:
        there = exists(a, b)
        total = total + there.astype(jnp.int32)

        @pl.when(there)
        def _(a=a, b=b):
            pl.semaphore_signal(barrier, inc=1, device_id=(s + a, q + b), device_id_type=MESH)

    pl.semaphore_wait(barrier, total)

    def copies(a, b):
        back = slot_of(-a, -b)
        out = [
            pltpu.make_async_remote_copy(
                src_ref=packet,
                dst_ref=packets.at[back],
                send_sem=send_sem.at[0, slot_of(a, b)],
                recv_sem=recv_sem.at[0, back],
                device_id=(s + a, q + b),
                device_id_type=MESH,
            )
        ]
        if with_target:
            x0, x1, y0, y1 = target_piece(-a, -b, bx, by)
            X = 6 - a * bx + x0
            Y = 8 - b * by + y0
            out.append(
                pltpu.make_async_remote_copy(
                    src_ref=target.at[x0:x1, y0:y1],
                    dst_ref=wide.at[X : X + x1 - x0, Y : Y + y1 - y0],
                    send_sem=send_sem.at[1, slot_of(a, b)],
                    recv_sem=recv_sem.at[1, back],
                    device_id=(s + a, q + b),
                    device_id_type=MESH,
                )
            )
            out.append(
                pltpu.make_async_remote_copy(
                    src_ref=count,
                    dst_ref=counts.at[back],
                    send_sem=send_sem.at[2, slot_of(a, b)],
                    recv_sem=recv_sem.at[2, back],
                    device_id=(s + a, q + b),
                    device_id_type=MESH,
                )
            )
        return out

    def arrivals(a, b):
        mine = slot_of(a, b)
        out = [
            pltpu.make_async_remote_copy(
                src_ref=packet,
                dst_ref=packets.at[mine],
                send_sem=send_sem.at[0, mine],
                recv_sem=recv_sem.at[0, mine],
                device_id=(s + a, q + b),
                device_id_type=MESH,
            )
        ]
        if with_target:
            x0, x1, y0, y1 = target_piece(a, b, bx, by)
            X = 6 + a * bx + x0
            Y = 8 + b * by + y0
            out.append(
                pltpu.make_async_remote_copy(
                    src_ref=target.at[x0:x1, y0:y1],
                    dst_ref=wide.at[X : X + x1 - x0, Y : Y + y1 - y0],
                    send_sem=send_sem.at[1, mine],
                    recv_sem=recv_sem.at[1, mine],
                    device_id=(s + a, q + b),
                    device_id_type=MESH,
                )
            )
            out.append(
                pltpu.make_async_remote_copy(
                    src_ref=count,
                    dst_ref=counts.at[mine],
                    send_sem=send_sem.at[2, mine],
                    recv_sem=recv_sem.at[2, mine],
                    device_id=(s + a, q + b),
                    device_id_type=MESH,
                )
            )
        return out

    for a, b in NEIGHBOURS:

        @pl.when(exists(a, b))
        def _(a=a, b=b):
            for c in copies(a, b):
                c.start()

    for a, b in NEIGHBOURS:

        @pl.when(exists(a, b))
        def _(a=a, b=b):
            for c in arrivals(a, b):
                c.wait_recv()
            for c in copies(a, b):
                c.wait_send()


def exchange(packet, target, count, bx, by, gz, cid):
    with_target = target is not None
    out_shape = [jax.ShapeDtypeStruct((SLOTS,) + packet.shape, F32)]
    operands = [packet]
    if with_target:
        out_shape.append(jax.ShapeDtypeStruct((bx + 13, by + 16, gz), F32))
        out_shape.append(jax.ShapeDtypeStruct((SLOTS,) + count.shape, F32))
        operands.extend([target, count])
    return pl.pallas_call(
        functools.partial(exchange_kernel, with_target, bx, by),
        out_shape=out_shape,
        in_specs=[ANY] * len(operands),
        out_specs=[ANY] * len(out_shape),
        scratch_shapes=[
            pltpu.SemaphoreType.DMA((3, SLOTS)),
            pltpu.SemaphoreType.DMA((3, SLOTS)),
        ],
        compiler_params=pltpu.CompilerParams(collective_id=cid, has_side_effects=True),
        name="exchange%d" % cid,
    )(*operands)


def split2(x):
    hi = x.astype(BF16)
    return hi, (x - hi.astype(F32)).astype(BF16)


def split3(x):
    hi = x.astype(BF16)
    rest = x - hi.astype(F32)
    mid = rest.astype(BF16)
    return hi, mid, (rest - mid.astype(F32)).astype(BF16)


def dot_nn(x, y):
    return lax.dot_general(x, y, (((1,), (0,)), ((), ())), preferred_element_type=F32)


def dot_nt(x, y):
    return lax.dot_general(x, y, (((1,), (1,)), ((), ())), preferred_element_type=F32)


def iota_f(shape, dim):
    return lax.broadcasted_iota(jnp.int32, shape, dim).astype(F32)


def tap_of(t):
    u = jnp.abs(t)
    return jnp.where(
        u == 0.0, TAPS[2], jnp.where(u == 1.0, TAPS[1], jnp.where(u == 2.0, TAPS[0], 0.0))
    )


def z_weights(iz, az, lower, upper):
    low_h, low_l = split2(lower)
    up_h, up_l = split2(upper)
    at_low = iz == az.astype(BF16)
    at_up = iz == (az + 1.0).astype(BF16)
    zero = jnp.zeros((), BF16)
    high = jnp.where(at_low, low_h, jnp.where(at_up, up_h, zero))
    return high, jnp.where(at_low, low_l, jnp.where(at_up, up_l, zero))


def band(gz, radius, taps):
    i = lax.broadcasted_iota(jnp.int32, (gz, gz), 0)
    j = lax.broadcasted_iota(jnp.int32, (gz, gz), 1)
    t = (i - j).astype(F32)
    if taps:
        return tap_of(t).astype(BF16)
    return jnp.where(jnp.abs(t) <= radius, 1.0, 0.0).astype(BF16)


def pack_kernel(fraction, anchor, kinds, counts, table, packet, mass, count):
    atoms = packet.shape[1]
    n = counts[0, 0]
    kind = kinds[0]
    lane = lax.broadcasted_iota(jnp.int32, (1, atoms), 1)
    rows = []
    for r in range(3):
        row = jnp.zeros((1, atoms), F32)
        for t in range(table.shape[1]):
            row = jnp.where(kind == t, table[r, t], row)
        rows.append(row)
    packet[0:3] = anchor[:, 0, 0, :].astype(F32)
    packet[3:6] = fraction[:, 0, 0, :]
    packet[6:7] = jnp.where(lane < n, rows[0], 0.0)
    packet[7:8] = rows[1] * rows[1]
    mass[...] = rows[2]
    count[...] = jnp.full(count.shape, n.astype(F32))


SPREAD = -2.0 / math.log2(math.e)


def step_kernel(first, last, bx, by, gz, n_x, n_y, *refs):
    if first:
        (own_count, counts, packets, own_packet, mass, velocity, wide, target,
         vel_out, moved_out, next_packet, pot, inv_ref, tgt_ref,
         pk, pos, feat, cols, acc, dens, tile1, other1, tile2, other2, wm) = refs
    else:
        (own_count, counts, packets, own_packet, mass, velocity, moved, inv_ref, tgt_ref,
         vel_out, moved_out, pot,
         pk, pos, feat, cols, acc, dens, tile1, other1, tile2, other2) = refs
    atoms = own_packet.shape[1]
    s, q = lax.axis_index("cells"), lax.axis_index("grp")
    rx, ry = bx + 5, by + 8
    own_live = own_count[0, 0]

    def live_in(slot, a, b):
        n = jnp.where(exists(a, b), counts[slot, 0, 0].astype(jnp.int32), 0)
        return jnp.where(slot == OWN, own_live, n)

    row = lax.broadcasted_iota(jnp.int32, (8, atoms), 0)
    for a in range(-RX, RX + 1):
        for b in range(-RY, RY + 1):
            slot = slot_of(a, b)
            if slot == OWN:
                block = own_packet[...]
            else:
                block = jnp.where(exists(a, b), packets[slot], 0.0)
            pk[slot] = block
            if abs(a) <= 1:
                base = jnp.where(row == 0, float(a * bx), jnp.where(row == 1, float(b * by), 0.0))
                place = jnp.where(
                    row < 3, block + pltpu.roll(block, 5, 0) + base, pltpu.roll(block, 4, 0) * SPREAD
                )
                pos[slot] = place
                four = jnp.where(row < 3, place, jnp.where(row == 3, 1.0, 0.0)) * block[6:7]
                h, m, l = split3(four)
                feat[slot] = jnp.concatenate(
                    [h.astype(F32), m.astype(F32), l.astype(F32), jnp.zeros_like(four)], 0
                )

    own_t = jnp.transpose(pos[OWN])
    for k in range(4):
        cols[k] = jnp.broadcast_to(own_t[:, k : k + 1], (atoms, 128))
    acc[...] = jnp.zeros_like(acc)
    half = atoms // 2

    def pairs(height):
        rows = pl.ds(0, height)

        def add(tile, other_tile):
            acc[rows] += dot_nt(tile[rows], other_tile[...])

        def compute(slot, start, width, tile, other_tile):
            add(tile, other_tile)
            for k in range(0, width, 128):
                at = pl.ds(pl.multiple_of(start + k, 128), 128)
                other = pos[slot, :, at]
                dx = cols[0, rows] - other[0:1]
                dy = cols[1, rows] - other[1:2]
                dz = cols[2, rows] - other[2:3]
                d2 = dx * dx + dy * dy + dz * dz
                inverse = 1.0 / (cols[3, rows] + other[3:4])
                value = jnp.exp2(d2 * inverse) * inverse
                hi, lo = split2(value)
                tile[rows, 2 * k : 2 * k + 128] = hi
                tile[rows, 2 * k + 128 : 2 * k + 256] = lo
                f = feat[slot, :, at].astype(BF16)
                other_tile[:, 2 * k : 2 * k + 128] = f
                other_tile[:, 2 * k + 128 : 2 * k + 256] = f

        def per_slot(slot, carry):
            n = live_in(slot, slot // NB - RX, slot % NB - RY)
            blocks = (n + 127) // 128

            def per_block(block, carry):
                compute(slot, block * 256, 256, tile2, other2)
                return carry

            lax.fori_loop(0, blocks // 2, per_block, 0)

            @pl.when(blocks % 2 == 1)
            def _():
                compute(slot, (blocks // 2) * 256, 128, tile1, other1)

            return carry

        for ref in (tile1, other1, tile2, other2):
            ref[...] = jnp.zeros_like(ref)
        lax.fori_loop(NB * (RX - 1), NB * (RX + 2), per_slot, 0)
        add(tile1, other1)
        add(tile2, other2)

    @pl.when(own_live <= half)
    def _():
        pairs(half)

    @pl.when(own_live > half)
    def _():
        pairs(atoms)

    iz = iota_f((gz, half), 0).astype(BF16)

    def spread(a, b, start):
        p0 = max(0, a * bx)
        p1 = min(rx, a * bx + bx + 5)
        r0, r1 = {-1: (0, 8), 0: (0, ry), 1: (by, ry)}[b]
        block = pk[slot_of(a, b), :, start : start + half]
        charge = block[6:7]
        ax, ay, az = block[0:1], block[1:2], block[2:3]
        fx, fy, fz = block[3:4], block[4:5], block[5:6]
        ax = ax + float(a * bx)
        ay = ay + float(b * by)
        in_x = ax + 1.0 + (s * bx).astype(F32) < float(n_x)
        in_y = ay + 1.0 + (q * by).astype(F32) < float(n_y)
        ux = jnp.where(in_x, fx, 0.0)
        uy = jnp.where(in_y, fy, 0.0)
        tx = iota_f((p1 - p0, half), 0) + float(p0 - 2) - ax
        wx = tap_of(tx) * (1.0 - fx) + tap_of(tx - 1.0) * ux
        ty = iota_f((r1 - r0, half), 0) + float(r0 - 2) - ay
        wy = tap_of(ty) * (1.0 - fy) + tap_of(ty - 1.0) * uy
        plane = jnp.concatenate([wy * wx[p : p + 1] for p in range(p1 - p0)], 0)
        ph, plo = split2(plane)
        zh, zl = z_weights(iz, az, charge * (1.0 - fz), charge * fz)
        both = dot_nt(jnp.concatenate([ph, plo], 0), zh)
        size = plane.shape[0]
        summed = both[:size] + both[size:] + dot_nt(ph, zl)
        dens[p0:p1, r0:r1] += summed.reshape(p1 - p0, r1 - r0, gz)

    dens[...] = jnp.zeros_like(dens)
    cells = [(0, 0)] + list(NEIGHBOURS)
    for a, b in cells:
        spread(a, b, 0)
    for a, b in cells:

        @pl.when(live_in(slot_of(a, b), a, b) > half)
        def _(a=a, b=b):
            spread(a, b, half)

    blur_z = band(gz, 2, True)

    def z_blur(x):
        h, l = split2(x)
        size = x.shape[0]
        both = dot_nn(jnp.concatenate([h, l], 0), blur_z)
        return both[:size] + both[size:]

    gx = lax.broadcasted_iota(jnp.int32, (rx, ry, gz), 0) - 2 + s * bx
    gy = lax.broadcasted_iota(jnp.int32, (rx, ry, gz), 1) - 2 + q * by
    inside = (gx >= 0) & (gx < n_x) & (gy >= 0) & (gy < n_y)

    if first:
        wxp, wyp = bx + 13, by + 16
        tx = lax.broadcasted_iota(jnp.int32, (wxp, wyp, gz), 0) - 6 + s * bx
        ty = lax.broadcasted_iota(jnp.int32, (wxp, wyp, gz), 1) - 8 + q * by
        valid = (tx >= 0) & (tx < n_x) & (ty >= 0) & (ty < n_y)
        wm[...] = jnp.where(valid, wide[...], 0.0)
        wm[6 : 6 + bx, 8 : 8 + by] = target[...]
        t = wm[...]

        box_z = band(gz, 4, False)

        def boxed(v):
            two = v[:-1] + v[1:]
            four = two[:-2] + two[2:]
            eight = four[:-4] + four[4:]
            v = eight[:rx] + v[8 : 8 + rx]
            size = wyp
            two = v + pltpu.roll(v, size - 1, 1)
            four = two + pltpu.roll(two, size - 2, 1)
            eight = four + pltpu.roll(four, size - 4, 1)
            nine = eight + pltpu.roll(v, size - 8, 1)
            v = pltpu.roll(nine, size - 2, 1)[:, :ry]
            v = v.reshape(rx * ry, gz)
            h, m, l = split3(v)
            size = v.shape[0]
            out = dot_nn(jnp.concatenate([h, m, l], 0), box_z)
            out = out[:size] + out[size : 2 * size] + out[2 * size :]
            return out.reshape(rx, ry, gz) * (1.0 / 729.0)

        mean_one = boxed(t)
        mean_two = boxed(t * t)
        inverse_scale = lax.rsqrt(mean_two - mean_one * mean_one + EPSILON)
        inverse_scale = jnp.where(inside, inverse_scale, 0.0)
        near = pltpu.roll(t[4 : 4 + rx], wyp - 6, 1)[:, :ry]
        inv_ref[...] = inverse_scale
        tgt_ref[...] = near
    else:
        inverse_scale = inv_ref[...]
        near = tgt_ref[...]

    blurred = z_blur(dens[...].reshape(rx * ry, gz)).reshape(rx, ry, gz)
    residual = jnp.where(inside, (blurred - near) * inverse_scale, 0.0)
    along = TAPS[0] * (residual[0 : bx + 1] + residual[4 : bx + 5])
    along = along + TAPS[1] * (residual[1 : bx + 2] + residual[3 : bx + 4])
    along = along + TAPS[2] * residual[2 : bx + 3]
    down = TAPS[0] * along
    for k in range(1, 5):
        down = down + TAPS[k] * pltpu.roll(along, ry - k, 1)
    potential = z_blur(down.reshape((bx + 1) * ry, gz)).reshape(bx + 1, ry, gz)
    pot[...] = potential[:bx, :by]
    px = lax.broadcasted_iota(jnp.int32, (bx + 1, ry, gz), 0) + s * bx
    py = lax.broadcasted_iota(jnp.int32, (bx + 1, ry, gz), 1) + q * by
    py_local = lax.broadcasted_iota(jnp.int32, (bx + 1, ry, gz), 1)
    field = jnp.where((px < n_x) & (py < n_y) & (py_local <= by), potential, 0.0)

    own = pk[OWN]
    charge = own[6:7]
    ax, ay, az = own[0:1], own[1:2], own[2:3]
    fx, fy, fz = own[3:4], own[4:5], own[5:6]
    iz = iota_f((gz, atoms), 0).astype(BF16)
    zh, zl = z_weights(iz, az, charge * (1.0 - fz), charge * fz)
    gh, gl = z_weights(iz, az, -charge, charge)
    size = (bx + 1) * ry
    fh, fl = split2(field.reshape(size, gz))
    fboth = jnp.concatenate([fh, fl], 0)

    def sampled(h, l):
        both = dot_nn(fboth, h)
        return both[:size] + both[size:] + dot_nn(fh, l)

    value = sampled(zh, zl)
    slope = sampled(gh, gl)
    iy = iota_f((ry, atoms), 0)
    low_y = jnp.where(iy == ay, 1.0, 0.0)
    up_y = jnp.where(iy == ay + 1.0, 1.0, 0.0)
    wy = low_y * (1.0 - fy) + up_y * fy
    sy = up_y - low_y
    grad_x = jnp.zeros((1, atoms), F32)
    grad_y = jnp.zeros((1, atoms), F32)
    grad_z = jnp.zeros((1, atoms), F32)
    for p in range(bx + 1):
        low_x = jnp.where(ax == float(p), 1.0, 0.0)
        up_x = jnp.where(ax + 1.0 == float(p), 1.0, 0.0)
        wx = low_x * (1.0 - fx) + up_x * fx
        sx = up_x - low_x
        v = value[p * ry : (p + 1) * ry]
        g = slope[p * ry : (p + 1) * ry]
        grad_x = grad_x + sx * jnp.sum(wy * v, 0, keepdims=True)
        grad_y = grad_y + wx * jnp.sum(sy * v, 0, keepdims=True)
        grad_z = grad_z + wx * jnp.sum(wy * g, 0, keepdims=True)
    gradient = jnp.concatenate([grad_x, grad_y, grad_z], 0)

    sums = jnp.transpose(acc[...])
    sums = sums[0:8] + sums[8:16] + sums[16:24]
    here = pos[OWN][0:3]
    pair = (SPREAD * charge) * (here * sums[3:4] - sums[0:3])
    old_velocity = velocity[:, 0, 0, :] if first else velocity[...]
    new_velocity = old_velocity + TIME_STEP * (pair - gradient) / mass[...]
    new_moved = TIME_STEP * new_velocity
    if not first:
        new_moved = moved[...] + new_moved
    if last:
        live = lax.broadcasted_iota(jnp.int32, (3, atoms), 1) < own_live
        vel_out[:, 0, 0, :] = jnp.where(live, new_velocity, 0.0)
        moved_out[:, 0, 0, :] = jnp.where(live, new_moved, 0.0)
    else:
        vel_out[...] = new_velocity
        moved_out[...] = new_moved
        next_packet[...] = jnp.concatenate(
            [own[0:3], own[3:6] + TIME_STEP * new_velocity, own[6:8]], 0
        )


def step_call(first, last, sizes, operands, out_shape):
    bx, by, gz, n_x, n_y, atoms = sizes
    scratch = [
        pltpu.VMEM((SLOTS, 8, atoms), F32),
        pltpu.VMEM((SLOTS, 8, atoms), F32),
        pltpu.VMEM((SLOTS, 32, atoms), F32),
        pltpu.VMEM((4, atoms, 128), F32),
        pltpu.VMEM((atoms, 32), F32),
        pltpu.VMEM((bx + 5, by + 8, gz), F32),
        pltpu.VMEM((atoms, 256), BF16),
        pltpu.VMEM((32, 256), BF16),
        pltpu.VMEM((atoms, 512), BF16),
        pltpu.VMEM((32, 512), BF16),
    ]
    if first:
        scratch.append(pltpu.VMEM((bx + 13, by + 16, gz), F32))
    return pl.pallas_call(
        functools.partial(step_kernel, first, last, bx, by, gz, n_x, n_y),
        out_shape=out_shape,
        in_specs=[SMEM, SMEM] + [VMEM] * (len(operands) - 2),
        out_specs=[VMEM] * len(out_shape),
        scratch_shapes=scratch,
        name="first_step" if first else "last_step",
    )(*operands)


def per_device(fraction, velocity, anchor, atom_types, counts, type_table, target):
    atoms = fraction.shape[3]
    bx, by, gz = target.shape
    n_x = bx * lax.axis_size("cells")
    n_y = by * lax.axis_size("grp")
    packet, mass, count = pl.pallas_call(
        pack_kernel,
        out_shape=[
            jax.ShapeDtypeStruct((8, atoms), F32),
            jax.ShapeDtypeStruct((1, atoms), F32),
            jax.ShapeDtypeStruct((1, 128), F32),
        ],
        in_specs=[VMEM, VMEM, VMEM, SMEM, SMEM],
        out_specs=[VMEM] * 3,
        name="pack",
    )(fraction, anchor, atom_types, counts, type_table)
    packets, wide, near_counts = exchange(packet, target, count, bx, by, gz, 0)
    sizes = (bx, by, gz, n_x, n_y, atoms)
    row = jax.ShapeDtypeStruct((3, atoms), F32)
    final = jax.ShapeDtypeStruct(velocity.shape, F32)
    field = jax.ShapeDtypeStruct((bx, by, gz), F32)
    region = jax.ShapeDtypeStruct((bx + 5, by + 8, gz), F32)
    velocity, moved, next_packet, _, inverse, near = step_call(
        True, False, sizes,
        (counts, near_counts, packets, packet, mass, velocity, wide, target),
        [row, row, jax.ShapeDtypeStruct((8, atoms), F32), field, region, region],
    )
    (later,) = exchange(next_packet, None, None, bx, by, gz, 1)
    return tuple(
        step_call(
            False, True, sizes,
            (counts, near_counts, later, next_packet, mass, velocity, moved, inverse, near),
            [final, final, field],
        )
    )


def solution(mesh):
    placed = (
        P(None, "cells", "grp", None),
        P(None, "cells", "grp", None),
        P(None, "cells", "grp", None),
        P("cells", "grp", None),
        P("cells", "grp"),
        P(),
        P("cells", "grp", None),
    )
    return jax.shard_map(
        per_device,
        mesh=mesh,
        in_specs=placed,
        out_specs=(
            P(None, "cells", "grp", None),
            P(None, "cells", "grp", None),
            P("cells", "grp", None),
        ),
        check_vma=False,
    )
```

```python
import functools
import math

import jax
import jax.numpy as jnp
from jax import lax
from jax.experimental import pallas as pl
from jax.experimental.pallas import tpu as pltpu
from jax.sharding import PartitionSpec as P

EPSILON = 1e-06
TIME_STEP = 0.5
TAPS = (1.0 / 16.0, 4.0 / 16.0, 6.0 / 16.0, 4.0 / 16.0, 1.0 / 16.0)
F32 = jnp.float32
BF16 = jnp.bfloat16
RX, RY = 2, 1
NB = 2 * RY + 1
SLOTS = (2 * RX + 1) * NB
OWN = RX * NB + RY
MESH = pl.DeviceIdType.MESH
VMEM = pl.BlockSpec(memory_space=pltpu.VMEM)
SMEM = pl.BlockSpec(memory_space=pltpu.SMEM)
ANY = pl.BlockSpec(memory_space=pl.ANY)
NEIGHBOURS = tuple(
    (a, b) for a in range(-RX, RX + 1) for b in range(-RY, RY + 1) if (a, b) != (0, 0)
)


def slot_of(a, b):
    return (a + RX) * NB + (b + RY)


def exists(a, b):
    s = lax.axis_index("cells") + a
    q = lax.axis_index("grp") + b
    ns, nq = lax.axis_size("cells"), lax.axis_size("grp")
    return (s >= 0) & (s < ns) & (q >= 0) & (q < nq)


def target_piece(a, b, bx, by):
    x0 = max(0, -6 - a * bx)
    x1 = min(bx, bx + 7 - a * bx)
    y0, y1 = {-1: (by - 8, by), 0: (0, by), 1: (0, 8)}[b]
    return x0, x1, y0, y1


def exchange_kernel(with_target, bx, by, *refs):
    if with_target:
        (fraction, anchor, kinds, own_counts, table, target,
         packet, mass, count, packets, wide, counts, send_sem, recv_sem) = refs
    else:
        packet, packets, send_sem, recv_sem = refs
    s, q = lax.axis_index("cells"), lax.axis_index("grp")
    barrier = pltpu.get_barrier_semaphore()
    total = jnp.int32(0)
    for a, b in NEIGHBOURS:
        there = exists(a, b)
        total = total + there.astype(jnp.int32)

        @pl.when(there)
        def _(a=a, b=b):
            pl.semaphore_signal(barrier, inc=1, device_id=(s + a, q + b), device_id_type=MESH)

    if with_target:
        pack(fraction, anchor, kinds, own_counts, table, packet, mass, count)
    pl.semaphore_wait(barrier, total)

    def copies(a, b):
        back = slot_of(-a, -b)
        out = [
            pltpu.make_async_remote_copy(
                src_ref=packet,
                dst_ref=packets.at[back],
                send_sem=send_sem.at[0, slot_of(a, b)],
                recv_sem=recv_sem.at[0, back],
                device_id=(s + a, q + b),
                device_id_type=MESH,
            )
        ]
        if with_target:
            x0, x1, y0, y1 = target_piece(-a, -b, bx, by)
            X = 6 - a * bx + x0
            Y = 8 - b * by + y0
            out.append(
                pltpu.make_async_remote_copy(
                    src_ref=target.at[x0:x1, y0:y1],
                    dst_ref=wide.at[X : X + x1 - x0, Y : Y + y1 - y0],
                    send_sem=send_sem.at[1, slot_of(a, b)],
                    recv_sem=recv_sem.at[1, back],
                    device_id=(s + a, q + b),
                    device_id_type=MESH,
                )
            )
            out.append(
                pltpu.make_async_remote_copy(
                    src_ref=count,
                    dst_ref=counts.at[back],
                    send_sem=send_sem.at[2, slot_of(a, b)],
                    recv_sem=recv_sem.at[2, back],
                    device_id=(s + a, q + b),
                    device_id_type=MESH,
                )
            )
        return out

    def arrivals(a, b):
        mine = slot_of(a, b)
        out = [
            pltpu.make_async_remote_copy(
                src_ref=packet,
                dst_ref=packets.at[mine],
                send_sem=send_sem.at[0, mine],
                recv_sem=recv_sem.at[0, mine],
                device_id=(s + a, q + b),
                device_id_type=MESH,
            )
        ]
        if with_target:
            x0, x1, y0, y1 = target_piece(a, b, bx, by)
            X = 6 + a * bx + x0
            Y = 8 + b * by + y0
            out.append(
                pltpu.make_async_remote_copy(
                    src_ref=target.at[x0:x1, y0:y1],
                    dst_ref=wide.at[X : X + x1 - x0, Y : Y + y1 - y0],
                    send_sem=send_sem.at[1, mine],
                    recv_sem=recv_sem.at[1, mine],
                    device_id=(s + a, q + b),
                    device_id_type=MESH,
                )
            )
            out.append(
                pltpu.make_async_remote_copy(
                    src_ref=count,
                    dst_ref=counts.at[mine],
                    send_sem=send_sem.at[2, mine],
                    recv_sem=recv_sem.at[2, mine],
                    device_id=(s + a, q + b),
                    device_id_type=MESH,
                )
            )
        return out

    for a, b in NEIGHBOURS:

        @pl.when(exists(a, b))
        def _(a=a, b=b):
            for c in copies(a, b):
                c.start()

    for a, b in NEIGHBOURS:

        @pl.when(exists(a, b))
        def _(a=a, b=b):
            for c in arrivals(a, b):
                c.wait_recv()
            for c in copies(a, b):
                c.wait_send()


def exchange(operands, in_specs, out_shape, out_specs, bx, by, cid):
    return pl.pallas_call(
        functools.partial(exchange_kernel, cid == 0, bx, by),
        out_shape=out_shape,
        in_specs=in_specs,
        out_specs=out_specs,
        scratch_shapes=[
            pltpu.SemaphoreType.DMA((3, SLOTS)),
            pltpu.SemaphoreType.DMA((3, SLOTS)),
        ],
        compiler_params=pltpu.CompilerParams(collective_id=cid, has_side_effects=True),
        name="exchange%d" % cid,
    )(*operands)


def split2(x):
    hi = x.astype(BF16)
    return hi, (x - hi.astype(F32)).astype(BF16)


def split3(x):
    hi = x.astype(BF16)
    rest = x - hi.astype(F32)
    mid = rest.astype(BF16)
    return hi, mid, (rest - mid.astype(F32)).astype(BF16)


def dot_nn(x, y):
    return lax.dot_general(x, y, (((1,), (0,)), ((), ())), preferred_element_type=F32)


def dot_nt(x, y):
    return lax.dot_general(x, y, (((1,), (1,)), ((), ())), preferred_element_type=F32)


def iota_f(shape, dim):
    return lax.broadcasted_iota(jnp.int32, shape, dim).astype(F32)


def tap_of(t):
    u = jnp.abs(t)
    return jnp.where(
        u == 0.0, TAPS[2], jnp.where(u == 1.0, TAPS[1], jnp.where(u == 2.0, TAPS[0], 0.0))
    )


def z_weights(iz, az, lower, upper):
    low_h, low_l = split2(lower)
    up_h, up_l = split2(upper)
    at_low = iz == az.astype(BF16)
    at_up = iz == (az + 1.0).astype(BF16)
    zero = jnp.zeros((), BF16)
    high = jnp.where(at_low, low_h, jnp.where(at_up, up_h, zero))
    return high, jnp.where(at_low, low_l, jnp.where(at_up, up_l, zero))


def band(gz, radius, taps):
    i = lax.broadcasted_iota(jnp.int32, (gz, gz), 0)
    j = lax.broadcasted_iota(jnp.int32, (gz, gz), 1)
    t = (i - j).astype(F32)
    if taps:
        return tap_of(t).astype(BF16)
    return jnp.where(jnp.abs(t) <= radius, 1.0, 0.0).astype(BF16)


def pack(fraction, anchor, kinds, counts, table, packet, mass, count):
    atoms = packet.shape[1]
    n = counts[0, 0]
    kind = kinds[0]
    lane = lax.broadcasted_iota(jnp.int32, (1, atoms), 1)
    rows = []
    for r in range(3):
        row = jnp.zeros((1, atoms), F32)
        for t in range(table.shape[1]):
            row = jnp.where(kind == t, table[r, t], row)
        rows.append(row)
    packet[0:3] = anchor[:, 0, 0, :].astype(F32)
    packet[3:6] = fraction[:, 0, 0, :]
    packet[6:7] = jnp.where(lane < n, rows[0], 0.0)
    packet[7:8] = rows[1] * rows[1]
    mass[...] = rows[2]
    count[...] = jnp.full(count.shape, n.astype(F32))


SPREAD = -2.0 / math.log2(math.e)


def step_kernel(first, last, bx, by, gz, n_x, n_y, *refs):
    if first:
        (own_count, counts, packets, own_packet, mass, velocity, wide, target,
         vel_out, moved_out, next_fraction, pot, inv_ref, tgt_ref,
         pk, pos, feat, cols, acc, dens, tile1, other1, tile2, other2, wm) = refs
    else:
        (own_count, counts, packets, own_packet, mass, later, own_later,
         velocity, moved, inv_ref, tgt_ref,
         vel_out, moved_out, pot,
         pk, pos, feat, cols, acc, dens, tile1, other1, tile2, other2) = refs
    atoms = own_packet.shape[1]
    s, q = lax.axis_index("cells"), lax.axis_index("grp")
    rx, ry = bx + 5, by + 8
    own_live = own_count[0, 0]

    def live_in(slot, a, b):
        n = jnp.where(exists(a, b), counts[slot, 0, 0].astype(jnp.int32), 0)
        return jnp.where(slot == OWN, own_live, n)

    row = lax.broadcasted_iota(jnp.int32, (8, atoms), 0)
    for a in range(-RX, RX + 1):
        for b in range(-RY, RY + 1):
            slot = slot_of(a, b)
            block = own_packet[...] if slot == OWN else packets[slot]
            if not first:
                now = own_later[...] if slot == OWN else later[slot]
                block = jnp.concatenate([block[0:3], now, block[6:8]], 0)
            if slot != OWN:
                block = jnp.where(exists(a, b), block, 0.0)
            pk[slot] = block
            if abs(a) <= 1:
                base = jnp.where(row == 0, float(a * bx), jnp.where(row == 1, float(b * by), 0.0))
                place = jnp.where(
                    row < 3, block + pltpu.roll(block, 5, 0) + base, pltpu.roll(block, 4, 0) * SPREAD
                )
                pos[slot] = place
                four = jnp.where(row < 3, place, jnp.where(row == 3, 1.0, 0.0)) * block[6:7]
                h, m, l = split3(four)
                feat[slot] = jnp.concatenate(
                    [h.astype(F32), m.astype(F32), l.astype(F32), jnp.zeros_like(four)], 0
                )

    own_t = jnp.transpose(pos[OWN])
    for k in range(4):
        cols[k] = jnp.broadcast_to(own_t[:, k : k + 1], (atoms, 128))
    acc[...] = jnp.zeros_like(acc)
    half = atoms // 2

    def pairs(height):
        rows = pl.ds(0, height)

        def add(tile, other_tile):
            acc[rows] += dot_nt(tile[rows], other_tile[...])

        def compute(slot, start, width, tile, other_tile):
            add(tile, other_tile)
            for k in range(0, width, 128):
                at = pl.ds(pl.multiple_of(start + k, 128), 128)
                other = pos[slot, :, at]
                dx = cols[0, rows] - other[0:1]
                dy = cols[1, rows] - other[1:2]
                dz = cols[2, rows] - other[2:3]
                d2 = dx * dx + dy * dy + dz * dz
                inverse = 1.0 / (cols[3, rows] + other[3:4])
                value = jnp.exp2(d2 * inverse) * inverse
                hi, lo = split2(value)
                tile[rows, 2 * k : 2 * k + 128] = hi
                tile[rows, 2 * k + 128 : 2 * k + 256] = lo
                f = feat[slot, :, at].astype(BF16)
                other_tile[:, 2 * k : 2 * k + 128] = f
                other_tile[:, 2 * k + 128 : 2 * k + 256] = f

        def per_slot(slot, carry):
            n = live_in(slot, slot // NB - RX, slot % NB - RY)
            blocks = (n + 127) // 128

            def per_block(block, carry):
                compute(slot, block * 256, 256, tile2, other2)
                return carry

            lax.fori_loop(0, blocks // 2, per_block, 0)

            @pl.when(blocks % 2 == 1)
            def _():
                compute(slot, (blocks // 2) * 256, 128, tile1, other1)

            return carry

        for ref in (tile1, other1, tile2, other2):
            ref[...] = jnp.zeros_like(ref)
        lax.fori_loop(NB * (RX - 1), NB * (RX + 2), per_slot, 0)
        add(tile1, other1)
        add(tile2, other2)

    @pl.when(own_live <= half)
    def _():
        pairs(half)

    @pl.when(own_live > half)
    def _():
        pairs(atoms)

    iz = iota_f((gz, half), 0).astype(BF16)

    def spread(a, b, start):
        p0 = max(0, a * bx)
        p1 = min(rx, a * bx + bx + 5)
        r0, r1 = {-1: (0, 8), 0: (0, ry), 1: (by, ry)}[b]
        block = pk[slot_of(a, b), :, start : start + half]
        charge = block[6:7]
        ax, ay, az = block[0:1], block[1:2], block[2:3]
        fx, fy, fz = block[3:4], block[4:5], block[5:6]
        ax = ax + float(a * bx)
        ay = ay + float(b * by)
        in_x = ax + 1.0 + (s * bx).astype(F32) < float(n_x)
        in_y = ay + 1.0 + (q * by).astype(F32) < float(n_y)
        ux = jnp.where(in_x, fx, 0.0)
        uy = jnp.where(in_y, fy, 0.0)
        tx = iota_f((p1 - p0, half), 0) + float(p0 - 2) - ax
        wx = tap_of(tx) * (1.0 - fx) + tap_of(tx - 1.0) * ux
        ty = iota_f((r1 - r0, half), 0) + float(r0 - 2) - ay
        wy = tap_of(ty) * (1.0 - fy) + tap_of(ty - 1.0) * uy
        plane = jnp.concatenate([wy * wx[p : p + 1] for p in range(p1 - p0)], 0)
        ph, plo = split2(plane)
        zh, zl = z_weights(iz, az, charge * (1.0 - fz), charge * fz)
        both = dot_nt(jnp.concatenate([ph, plo], 0), zh)
        size = plane.shape[0]
        summed = both[:size] + both[size:] + dot_nt(ph, zl)
        dens[p0:p1, r0:r1] += summed.reshape(p1 - p0, r1 - r0, gz)

    dens[...] = jnp.zeros_like(dens)
    cells = [(0, 0)] + list(NEIGHBOURS)
    for a, b in cells:
        spread(a, b, 0)
    for a, b in cells:

        @pl.when(live_in(slot_of(a, b), a, b) > half)
        def _(a=a, b=b):
            spread(a, b, half)

    blur_z = band(gz, 2, True)

    def z_blur(x):
        h, l = split2(x)
        size = x.shape[0]
        both = dot_nn(jnp.concatenate([h, l], 0), blur_z)
        return both[:size] + both[size:]

    gx = lax.broadcasted_iota(jnp.int32, (rx, ry, gz), 0) - 2 + s * bx
    gy = lax.broadcasted_iota(jnp.int32, (rx, ry, gz), 1) - 2 + q * by
    inside = (gx >= 0) & (gx < n_x) & (gy >= 0) & (gy < n_y)

    if first:
        wxp, wyp = bx + 13, by + 16
        tx = lax.broadcasted_iota(jnp.int32, (wxp, wyp, gz), 0) - 6 + s * bx
        ty = lax.broadcasted_iota(jnp.int32, (wxp, wyp, gz), 1) - 8 + q * by
        valid = (tx >= 0) & (tx < n_x) & (ty >= 0) & (ty < n_y)
        wm[...] = jnp.where(valid, wide[...], 0.0)
        wm[6 : 6 + bx, 8 : 8 + by] = target[...]
        t = wm[...]

        box_z = band(gz, 4, False)

        def boxed(v):
            two = v[:-1] + v[1:]
            four = two[:-2] + two[2:]
            eight = four[:-4] + four[4:]
            v = eight[:rx] + v[8 : 8 + rx]
            size = wyp
            two = v + pltpu.roll(v, size - 1, 1)
            four = two + pltpu.roll(two, size - 2, 1)
            eight = four + pltpu.roll(four, size - 4, 1)
            nine = eight + pltpu.roll(v, size - 8, 1)
            v = pltpu.roll(nine, size - 2, 1)[:, :ry]
            v = v.reshape(rx * ry, gz)
            h, m, l = split3(v)
            size = v.shape[0]
            out = dot_nn(jnp.concatenate([h, m, l], 0), box_z)
            out = out[:size] + out[size : 2 * size] + out[2 * size :]
            return out.reshape(rx, ry, gz) * (1.0 / 729.0)

        mean_one = boxed(t)
        mean_two = boxed(t * t)
        inverse_scale = lax.rsqrt(mean_two - mean_one * mean_one + EPSILON)
        inverse_scale = jnp.where(inside, inverse_scale, 0.0)
        near = pltpu.roll(t[4 : 4 + rx], wyp - 6, 1)[:, :ry]
        inv_ref[...] = inverse_scale
        tgt_ref[...] = near
    else:
        inverse_scale = inv_ref[...]
        near = tgt_ref[...]

    blurred = z_blur(dens[...].reshape(rx * ry, gz)).reshape(rx, ry, gz)
    residual = jnp.where(inside, (blurred - near) * inverse_scale, 0.0)
    along = TAPS[0] * (residual[0 : bx + 1] + residual[4 : bx + 5])
    along = along + TAPS[1] * (residual[1 : bx + 2] + residual[3 : bx + 4])
    along = along + TAPS[2] * residual[2 : bx + 3]
    down = TAPS[0] * along
    for k in range(1, 5):
        down = down + TAPS[k] * pltpu.roll(along, ry - k, 1)
    potential = z_blur(down.reshape((bx + 1) * ry, gz)).reshape(bx + 1, ry, gz)
    pot[...] = potential[:bx, :by]
    px = lax.broadcasted_iota(jnp.int32, (bx + 1, ry, gz), 0) + s * bx
    py = lax.broadcasted_iota(jnp.int32, (bx + 1, ry, gz), 1) + q * by
    py_local = lax.broadcasted_iota(jnp.int32, (bx + 1, ry, gz), 1)
    field = jnp.where((px < n_x) & (py < n_y) & (py_local <= by), potential, 0.0)

    own = pk[OWN]
    charge = own[6:7]
    ax, ay, az = own[0:1], own[1:2], own[2:3]
    fx, fy, fz = own[3:4], own[4:5], own[5:6]
    iz = iota_f((gz, atoms), 0).astype(BF16)
    zh, zl = z_weights(iz, az, charge * (1.0 - fz), charge * fz)
    gh, gl = z_weights(iz, az, -charge, charge)
    size = (bx + 1) * ry
    fh, fl = split2(field.reshape(size, gz))
    fboth = jnp.concatenate([fh, fl], 0)

    def sampled(h, l):
        both = dot_nn(fboth, h)
        return both[:size] + both[size:] + dot_nn(fh, l)

    value = sampled(zh, zl)
    slope = sampled(gh, gl)
    iy = iota_f((ry, atoms), 0)
    low_y = jnp.where(iy == ay, 1.0, 0.0)
    up_y = jnp.where(iy == ay + 1.0, 1.0, 0.0)
    wy = low_y * (1.0 - fy) + up_y * fy
    sy = up_y - low_y
    grad_x = jnp.zeros((1, atoms), F32)
    grad_y = jnp.zeros((1, atoms), F32)
    grad_z = jnp.zeros((1, atoms), F32)
    for p in range(bx + 1):
        low_x = jnp.where(ax == float(p), 1.0, 0.0)
        up_x = jnp.where(ax + 1.0 == float(p), 1.0, 0.0)
        wx = low_x * (1.0 - fx) + up_x * fx
        sx = up_x - low_x
        v = value[p * ry : (p + 1) * ry]
        g = slope[p * ry : (p + 1) * ry]
        grad_x = grad_x + sx * jnp.sum(wy * v, 0, keepdims=True)
        grad_y = grad_y + wx * jnp.sum(sy * v, 0, keepdims=True)
        grad_z = grad_z + wx * jnp.sum(wy * g, 0, keepdims=True)
    gradient = jnp.concatenate([grad_x, grad_y, grad_z], 0)

    sums = jnp.transpose(acc[...])
    sums = sums[0:8] + sums[8:16] + sums[16:24]
    here = pos[OWN][0:3]
    pair = (SPREAD * charge) * (here * sums[3:4] - sums[0:3])
    old_velocity = velocity[:, 0, 0, :] if first else velocity[...]
    new_velocity = old_velocity + TIME_STEP * (pair - gradient) / mass[...]
    new_moved = TIME_STEP * new_velocity
    if not first:
        new_moved = moved[...] + new_moved
    if last:
        live = lax.broadcasted_iota(jnp.int32, (3, atoms), 1) < own_live
        vel_out[:, 0, 0, :] = jnp.where(live, new_velocity, 0.0)
        moved_out[:, 0, 0, :] = jnp.where(live, new_moved, 0.0)
    else:
        vel_out[...] = new_velocity
        moved_out[...] = new_moved
        next_fraction[...] = own[3:6] + TIME_STEP * new_velocity


def step_call(first, last, sizes, operands, out_shape):
    bx, by, gz, n_x, n_y, atoms = sizes
    scratch = [
        pltpu.VMEM((SLOTS, 8, atoms), F32),
        pltpu.VMEM((SLOTS, 8, atoms), F32),
        pltpu.VMEM((SLOTS, 32, atoms), F32),
        pltpu.VMEM((4, atoms, 128), F32),
        pltpu.VMEM((atoms, 32), F32),
        pltpu.VMEM((bx + 5, by + 8, gz), F32),
        pltpu.VMEM((atoms, 256), BF16),
        pltpu.VMEM((32, 256), BF16),
        pltpu.VMEM((atoms, 512), BF16),
        pltpu.VMEM((32, 512), BF16),
    ]
    if first:
        scratch.append(pltpu.VMEM((bx + 13, by + 16, gz), F32))
    return pl.pallas_call(
        functools.partial(step_kernel, first, last, bx, by, gz, n_x, n_y),
        out_shape=out_shape,
        in_specs=[SMEM, SMEM] + [VMEM] * (len(operands) - 2),
        out_specs=[VMEM] * len(out_shape),
        scratch_shapes=scratch,
        name="first_step" if first else "last_step",
    )(*operands)


def per_device(fraction, velocity, anchor, atom_types, counts, type_table, target):
    atoms = fraction.shape[3]
    bx, by, gz = target.shape
    n_x = bx * lax.axis_size("cells")
    n_y = by * lax.axis_size("grp")
    packet, mass, _, packets, wide, near_counts = exchange(
        (fraction, anchor, atom_types, counts, type_table, target),
        [VMEM, VMEM, VMEM, SMEM, SMEM, ANY],
        [
            jax.ShapeDtypeStruct((8, atoms), F32),
            jax.ShapeDtypeStruct((1, atoms), F32),
            jax.ShapeDtypeStruct((1, 128), F32),
            jax.ShapeDtypeStruct((SLOTS, 8, atoms), F32),
            jax.ShapeDtypeStruct((bx + 13, by + 16, gz), F32),
            jax.ShapeDtypeStruct((SLOTS, 1, 128), F32),
        ],
        [VMEM, VMEM, VMEM, ANY, ANY, ANY],
        bx, by, 0,
    )
    sizes = (bx, by, gz, n_x, n_y, atoms)
    row = jax.ShapeDtypeStruct((3, atoms), F32)
    final = jax.ShapeDtypeStruct(velocity.shape, F32)
    field = jax.ShapeDtypeStruct((bx, by, gz), F32)
    region = jax.ShapeDtypeStruct((bx + 5, by + 8, gz), F32)
    velocity, moved, moved_on, _, inverse, near = step_call(
        True, False, sizes,
        (counts, near_counts, packets, packet, mass, velocity, wide, target),
        [row, row, row, field, region, region],
    )
    (later,) = exchange(
        (moved_on,), [ANY], [jax.ShapeDtypeStruct((SLOTS, 3, atoms), F32)], [ANY], bx, by, 1
    )
    return tuple(
        step_call(
            False, True, sizes,
            (counts, near_counts, packets, packet, mass, later, moved_on, velocity, moved, inverse, near),
            [final, final, field],
        )
    )


def solution(mesh):
    placed = (
        P(None, "cells", "grp", None),
        P(None, "cells", "grp", None),
        P(None, "cells", "grp", None),
        P("cells", "grp", None),
        P("cells", "grp"),
        P(),
        P("cells", "grp", None),
    )
    return jax.shard_map(
        per_device,
        mesh=mesh,
        in_specs=placed,
        out_specs=(
            P(None, "cells", "grp", None),
            P(None, "cells", "grp", None),
            P("cells", "grp", None),
        ),
        check_vma=False,
    )
```

```python
import functools
import math

import jax
import jax.numpy as jnp
from jax import lax
from jax.experimental import pallas as pl
from jax.experimental.pallas import tpu as pltpu
from jax.sharding import PartitionSpec as P

EPSILON = 1e-06
TIME_STEP = 0.5
TAPS = (1.0 / 16.0, 4.0 / 16.0, 6.0 / 16.0, 4.0 / 16.0, 1.0 / 16.0)
F32 = jnp.float32
BF16 = jnp.bfloat16
RX, RY = 2, 1
NB = 2 * RY + 1
SLOTS = (2 * RX + 1) * NB
OWN = RX * NB + RY
MESH = pl.DeviceIdType.MESH
VMEM = pl.BlockSpec(memory_space=pltpu.VMEM)
SMEM = pl.BlockSpec(memory_space=pltpu.SMEM)
ANY = pl.BlockSpec(memory_space=pl.ANY)
NEIGHBOURS = tuple(
    (a, b) for b in (-RY, RY, 0) for a in range(-RX, RX + 1) if (a, b) != (0, 0)
)


def slot_of(a, b):
    return (a + RX) * NB + (b + RY)


def exists(a, b):
    s = lax.axis_index("cells") + a
    q = lax.axis_index("grp") + b
    ns, nq = lax.axis_size("cells"), lax.axis_size("grp")
    return (s >= 0) & (s < ns) & (q >= 0) & (q < nq)


def target_piece(a, b, bx, by):
    x0 = max(0, -6 - a * bx)
    x1 = min(bx, bx + 7 - a * bx)
    y0, y1 = {-1: (by - 8, by), 0: (0, by), 1: (0, 8)}[b]
    return x0, x1, y0, y1


def exchange_kernel(with_target, bx, by, *refs):
    if with_target:
        (fraction, anchor, kinds, own_counts, table, target,
         packet, mass, count, packets, wide, counts, send_sem, recv_sem) = refs
    else:
        packet, packets, send_sem, recv_sem = refs
    s, q = lax.axis_index("cells"), lax.axis_index("grp")
    barrier = pltpu.get_barrier_semaphore()
    total = jnp.int32(0)
    for a, b in NEIGHBOURS:
        there = exists(a, b)
        total = total + there.astype(jnp.int32)

        @pl.when(there)
        def _(a=a, b=b):
            pl.semaphore_signal(barrier, inc=1, device_id=(s + a, q + b), device_id_type=MESH)

    if with_target:
        pack(fraction, anchor, kinds, own_counts, table, packet, mass, count)
    pl.semaphore_wait(barrier, total)

    def copies(a, b):
        back = slot_of(-a, -b)
        out = [
            pltpu.make_async_remote_copy(
                src_ref=packet,
                dst_ref=packets.at[back],
                send_sem=send_sem.at[0, slot_of(a, b)],
                recv_sem=recv_sem.at[0, back],
                device_id=(s + a, q + b),
                device_id_type=MESH,
            )
        ]
        if with_target:
            x0, x1, y0, y1 = target_piece(-a, -b, bx, by)
            X = 6 - a * bx + x0
            Y = 8 - b * by + y0
            out.append(
                pltpu.make_async_remote_copy(
                    src_ref=target.at[x0:x1, y0:y1],
                    dst_ref=wide.at[X : X + x1 - x0, Y : Y + y1 - y0],
                    send_sem=send_sem.at[1, slot_of(a, b)],
                    recv_sem=recv_sem.at[1, back],
                    device_id=(s + a, q + b),
                    device_id_type=MESH,
                )
            )
            out.append(
                pltpu.make_async_remote_copy(
                    src_ref=count,
                    dst_ref=counts.at[back],
                    send_sem=send_sem.at[2, slot_of(a, b)],
                    recv_sem=recv_sem.at[2, back],
                    device_id=(s + a, q + b),
                    device_id_type=MESH,
                )
            )
        return out

    def arrivals(a, b):
        mine = slot_of(a, b)
        out = [
            pltpu.make_async_remote_copy(
                src_ref=packet,
                dst_ref=packets.at[mine],
                send_sem=send_sem.at[0, mine],
                recv_sem=recv_sem.at[0, mine],
                device_id=(s + a, q + b),
                device_id_type=MESH,
            )
        ]
        if with_target:
            x0, x1, y0, y1 = target_piece(a, b, bx, by)
            X = 6 + a * bx + x0
            Y = 8 + b * by + y0
            out.append(
                pltpu.make_async_remote_copy(
                    src_ref=target.at[x0:x1, y0:y1],
                    dst_ref=wide.at[X : X + x1 - x0, Y : Y + y1 - y0],
                    send_sem=send_sem.at[1, mine],
                    recv_sem=recv_sem.at[1, mine],
                    device_id=(s + a, q + b),
                    device_id_type=MESH,
                )
            )
            out.append(
                pltpu.make_async_remote_copy(
                    src_ref=count,
                    dst_ref=counts.at[mine],
                    send_sem=send_sem.at[2, mine],
                    recv_sem=recv_sem.at[2, mine],
                    device_id=(s + a, q + b),
                    device_id_type=MESH,
                )
            )
        return out

    for a, b in NEIGHBOURS:

        @pl.when(exists(a, b))
        def _(a=a, b=b):
            for c in copies(a, b):
                c.start()

    for a, b in NEIGHBOURS:

        @pl.when(exists(a, b))
        def _(a=a, b=b):
            for c in arrivals(a, b):
                c.wait_recv()
            for c in copies(a, b):
                c.wait_send()


def exchange(operands, in_specs, out_shape, out_specs, bx, by, cid):
    return pl.pallas_call(
        functools.partial(exchange_kernel, cid == 0, bx, by),
        out_shape=out_shape,
        in_specs=in_specs,
        out_specs=out_specs,
        scratch_shapes=[
            pltpu.SemaphoreType.DMA((3, SLOTS)),
            pltpu.SemaphoreType.DMA((3, SLOTS)),
        ],
        compiler_params=pltpu.CompilerParams(collective_id=cid, has_side_effects=True),
        name="exchange%d" % cid,
    )(*operands)


def split2(x):
    hi = x.astype(BF16)
    return hi, (x - hi.astype(F32)).astype(BF16)


def split3(x):
    hi = x.astype(BF16)
    rest = x - hi.astype(F32)
    mid = rest.astype(BF16)
    return hi, mid, (rest - mid.astype(F32)).astype(BF16)


def dot_nn(x, y):
    return lax.dot_general(x, y, (((1,), (0,)), ((), ())), preferred_element_type=F32)


def dot_nt(x, y):
    return lax.dot_general(x, y, (((1,), (1,)), ((), ())), preferred_element_type=F32)


def iota_f(shape, dim):
    return lax.broadcasted_iota(jnp.int32, shape, dim).astype(F32)


def tap_of(t):
    u = jnp.abs(t)
    return jnp.where(
        u == 0.0, TAPS[2], jnp.where(u == 1.0, TAPS[1], jnp.where(u == 2.0, TAPS[0], 0.0))
    )


def z_weights(iz, az, lower, upper):
    low_h, low_l = split2(lower)
    up_h, up_l = split2(upper)
    at_low = iz == az.astype(BF16)
    at_up = iz == (az + 1.0).astype(BF16)
    zero = jnp.zeros((), BF16)
    high = jnp.where(at_low, low_h, jnp.where(at_up, up_h, zero))
    return high, jnp.where(at_low, low_l, jnp.where(at_up, up_l, zero))


def band(gz, radius, taps):
    i = lax.broadcasted_iota(jnp.int32, (gz, gz), 0)
    j = lax.broadcasted_iota(jnp.int32, (gz, gz), 1)
    t = (i - j).astype(F32)
    if taps:
        return tap_of(t).astype(BF16)
    return jnp.where(jnp.abs(t) <= radius, 1.0, 0.0).astype(BF16)


def pack(fraction, anchor, kinds, counts, table, packet, mass, count):
    atoms = packet.shape[1]
    n = counts[0, 0]
    kind = kinds[0]
    lane = lax.broadcasted_iota(jnp.int32, (1, atoms), 1)
    rows = []
    for r in range(3):
        row = jnp.zeros((1, atoms), F32)
        for t in range(table.shape[1]):
            row = jnp.where(kind == t, table[r, t], row)
        rows.append(row)
    packet[0:3] = anchor[:, 0, 0, :].astype(F32)
    packet[3:6] = fraction[:, 0, 0, :]
    packet[6:7] = jnp.where(lane < n, rows[0], 0.0)
    packet[7:8] = rows[1] * rows[1]
    mass[...] = rows[2]
    count[...] = jnp.full(count.shape, n.astype(F32))


SPREAD = -2.0 / math.log2(math.e)


def step_kernel(first, last, bx, by, gz, n_x, n_y, *refs):
    if first:
        (own_count, counts, packets, own_packet, mass, velocity, wide, target,
         vel_out, moved_out, next_fraction, inv_ref, tgt_ref,
         pk, pos, feat, cols, acc, dens, tile1, other1, tile2, other2, wm) = refs
    else:
        (own_count, counts, packets, own_packet, mass, later, own_later,
         velocity, moved, inv_ref, tgt_ref,
         vel_out, moved_out, pot,
         pk, pos, feat, cols, acc, dens, tile1, other1, tile2, other2) = refs
    atoms = own_packet.shape[1]
    s, q = lax.axis_index("cells"), lax.axis_index("grp")
    rx, ry = bx + 5, by + 8
    own_live = own_count[0, 0]

    def live_in(slot, a, b):
        n = jnp.where(exists(a, b), counts[slot, 0, 0].astype(jnp.int32), 0)
        return jnp.where(slot == OWN, own_live, n)

    row = lax.broadcasted_iota(jnp.int32, (8, atoms), 0)
    for a in range(-RX, RX + 1):
        for b in range(-RY, RY + 1):
            slot = slot_of(a, b)
            block = own_packet[...] if slot == OWN else packets[slot]
            if not first:
                now = own_later[...] if slot == OWN else later[slot]
                block = jnp.concatenate([block[0:3], now, block[6:8]], 0)
            if slot != OWN:
                block = jnp.where(exists(a, b), block, 0.0)
            pk[slot] = block
            if abs(a) <= 1:
                base = jnp.where(row == 0, float(a * bx), jnp.where(row == 1, float(b * by), 0.0))
                place = jnp.where(
                    row < 3, block + pltpu.roll(block, 5, 0) + base, pltpu.roll(block, 4, 0) * SPREAD
                )
                pos[slot] = place
                four = jnp.where(row < 3, place, jnp.where(row == 3, 1.0, 0.0)) * block[6:7]
                h, m, l = split3(four)
                feat[slot] = jnp.concatenate(
                    [h.astype(F32), m.astype(F32), l.astype(F32), jnp.zeros_like(four)], 0
                )

    own_t = jnp.transpose(pos[OWN])
    for k in range(4):
        cols[k] = jnp.broadcast_to(own_t[:, k : k + 1], (atoms, 128))
    acc[...] = jnp.zeros_like(acc)
    half = atoms // 2

    def pairs(height):
        rows = pl.ds(0, height)

        def add(tile, other_tile):
            acc[rows] += dot_nt(tile[rows], other_tile[...])

        def compute(slot, start, width, tile, other_tile):
            add(tile, other_tile)
            for k in range(0, width, 128):
                at = pl.ds(pl.multiple_of(start + k, 128), 128)
                other = pos[slot, :, at]
                dx = cols[0, rows] - other[0:1]
                dy = cols[1, rows] - other[1:2]
                dz = cols[2, rows] - other[2:3]
                d2 = dx * dx + dy * dy + dz * dz
                inverse = 1.0 / (cols[3, rows] + other[3:4])
                value = jnp.exp2(d2 * inverse) * inverse
                hi, lo = split2(value)
                tile[rows, 2 * k : 2 * k + 128] = hi
                tile[rows, 2 * k + 128 : 2 * k + 256] = lo
                f = feat[slot, :, at].astype(BF16)
                other_tile[:, 2 * k : 2 * k + 128] = f
                other_tile[:, 2 * k + 128 : 2 * k + 256] = f

        def per_slot(slot, carry):
            n = live_in(slot, slot // NB - RX, slot % NB - RY)
            blocks = (n + 127) // 128

            def per_block(block, carry):
                compute(slot, block * 256, 256, tile2, other2)
                return carry

            lax.fori_loop(0, blocks // 2, per_block, 0)

            @pl.when(blocks % 2 == 1)
            def _():
                compute(slot, (blocks // 2) * 256, 128, tile1, other1)

            return carry

        for ref in (tile1, other1, tile2, other2):
            ref[...] = jnp.zeros_like(ref)
        lax.fori_loop(NB * (RX - 1), NB * (RX + 2), per_slot, 0)
        add(tile1, other1)
        add(tile2, other2)

    @pl.when(own_live <= half)
    def _():
        pairs(half)

    @pl.when(own_live > half)
    def _():
        pairs(atoms)

    iz = iota_f((gz, half), 0).astype(BF16)

    def spread(a, b, start):
        p0 = max(0, a * bx)
        p1 = min(rx, a * bx + bx + 5)
        r0, r1 = {-1: (0, 8), 0: (0, ry), 1: (by, ry)}[b]
        block = pk[slot_of(a, b), :, start : start + half]
        charge = block[6:7]
        ax, ay, az = block[0:1], block[1:2], block[2:3]
        fx, fy, fz = block[3:4], block[4:5], block[5:6]
        ax = ax + float(a * bx)
        ay = ay + float(b * by)
        in_x = ax + 1.0 + (s * bx).astype(F32) < float(n_x)
        in_y = ay + 1.0 + (q * by).astype(F32) < float(n_y)
        ux = jnp.where(in_x, fx, 0.0)
        uy = jnp.where(in_y, fy, 0.0)
        tx = iota_f((p1 - p0, half), 0) + float(p0 - 2) - ax
        wx = tap_of(tx) * (1.0 - fx) + tap_of(tx - 1.0) * ux
        ty = iota_f((r1 - r0, half), 0) + float(r0 - 2) - ay
        wy = tap_of(ty) * (1.0 - fy) + tap_of(ty - 1.0) * uy
        plane = jnp.concatenate([wy * wx[p : p + 1] for p in range(p1 - p0)], 0)
        ph, plo = split2(plane)
        zh, zl = z_weights(iz, az, charge * (1.0 - fz), charge * fz)
        both = dot_nt(jnp.concatenate([ph, plo], 0), zh)
        size = plane.shape[0]
        summed = both[:size] + both[size:] + dot_nt(ph, zl)
        dens[p0:p1, r0:r1] += summed.reshape(p1 - p0, r1 - r0, gz)

    dens[...] = jnp.zeros_like(dens)
    cells = [(0, 0)] + list(NEIGHBOURS)
    for a, b in cells:
        spread(a, b, 0)
    for a, b in cells:

        @pl.when(live_in(slot_of(a, b), a, b) > half)
        def _(a=a, b=b):
            spread(a, b, half)

    blur_z = band(gz, 2, True)

    def z_blur(x):
        h, l = split2(x)
        size = x.shape[0]
        both = dot_nn(jnp.concatenate([h, l], 0), blur_z)
        return both[:size] + both[size:]

    gx = lax.broadcasted_iota(jnp.int32, (rx, ry, gz), 0) - 2 + s * bx
    gy = lax.broadcasted_iota(jnp.int32, (rx, ry, gz), 1) - 2 + q * by
    inside = (gx >= 0) & (gx < n_x) & (gy >= 0) & (gy < n_y)

    if first:
        wxp, wyp = bx + 13, by + 16
        tx = lax.broadcasted_iota(jnp.int32, (wxp, wyp, gz), 0) - 6 + s * bx
        ty = lax.broadcasted_iota(jnp.int32, (wxp, wyp, gz), 1) - 8 + q * by
        valid = (tx >= 0) & (tx < n_x) & (ty >= 0) & (ty < n_y)
        wm[...] = jnp.where(valid, wide[...], 0.0)
        wm[6 : 6 + bx, 8 : 8 + by] = target[...]
        t = wm[...]

        box_z = band(gz, 4, False)

        def boxed(v):
            two = v[:-1] + v[1:]
            four = two[:-2] + two[2:]
            eight = four[:-4] + four[4:]
            v = eight[:rx] + v[8 : 8 + rx]
            size = wyp
            two = v + pltpu.roll(v, size - 1, 1)
            four = two + pltpu.roll(two, size - 2, 1)
            eight = four + pltpu.roll(four, size - 4, 1)
            nine = eight + pltpu.roll(v, size - 8, 1)
            v = pltpu.roll(nine, size - 2, 1)[:, :ry]
            v = v.reshape(rx * ry, gz)
            h, m, l = split3(v)
            size = v.shape[0]
            out = dot_nn(jnp.concatenate([h, m, l], 0), box_z)
            out = out[:size] + out[size : 2 * size] + out[2 * size :]
            return out.reshape(rx, ry, gz) * (1.0 / 729.0)

        mean_one = boxed(t)
        mean_two = boxed(t * t)
        inverse_scale = lax.rsqrt(mean_two - mean_one * mean_one + EPSILON)
        inverse_scale = jnp.where(inside, inverse_scale, 0.0)
        near = pltpu.roll(t[4 : 4 + rx], wyp - 6, 1)[:, :ry]
        inv_ref[...] = inverse_scale
        tgt_ref[...] = near
    else:
        inverse_scale = inv_ref[...]
        near = tgt_ref[...]

    blurred = z_blur(dens[...].reshape(rx * ry, gz)).reshape(rx, ry, gz)
    residual = jnp.where(inside, (blurred - near) * inverse_scale, 0.0)
    along = TAPS[0] * (residual[0 : bx + 1] + residual[4 : bx + 5])
    along = along + TAPS[1] * (residual[1 : bx + 2] + residual[3 : bx + 4])
    along = along + TAPS[2] * residual[2 : bx + 3]
    down = TAPS[0] * along
    for k in range(1, 5):
        down = down + TAPS[k] * pltpu.roll(along, ry - k, 1)
    potential = z_blur(down.reshape((bx + 1) * ry, gz)).reshape(bx + 1, ry, gz)
    if last:
        pot[...] = potential[:bx, :by]
    px = lax.broadcasted_iota(jnp.int32, (bx + 1, ry, gz), 0) + s * bx
    py = lax.broadcasted_iota(jnp.int32, (bx + 1, ry, gz), 1) + q * by
    py_local = lax.broadcasted_iota(jnp.int32, (bx + 1, ry, gz), 1)
    field = jnp.where((px < n_x) & (py < n_y) & (py_local <= by), potential, 0.0)

    own = pk[OWN]
    charge = own[6:7]
    ax, ay, az = own[0:1], own[1:2], own[2:3]
    fx, fy, fz = own[3:4], own[4:5], own[5:6]
    iz = iota_f((gz, atoms), 0).astype(BF16)
    zh, zl = z_weights(iz, az, charge * (1.0 - fz), charge * fz)
    gh, gl = z_weights(iz, az, -charge, charge)
    size = (bx + 1) * ry
    fh, fl = split2(field.reshape(size, gz))
    fboth = jnp.concatenate([fh, fl], 0)

    def sampled(h, l):
        both = dot_nn(fboth, h)
        return both[:size] + both[size:] + dot_nn(fh, l)

    value = sampled(zh, zl)
    slope = sampled(gh, gl)
    iy = iota_f((ry, atoms), 0)
    low_y = jnp.where(iy == ay, 1.0, 0.0)
    up_y = jnp.where(iy == ay + 1.0, 1.0, 0.0)
    wy = low_y * (1.0 - fy) + up_y * fy
    sy = up_y - low_y
    grad_x = jnp.zeros((1, atoms), F32)
    grad_y = jnp.zeros((1, atoms), F32)
    grad_z = jnp.zeros((1, atoms), F32)
    for p in range(bx + 1):
        low_x = jnp.where(ax == float(p), 1.0, 0.0)
        up_x = jnp.where(ax + 1.0 == float(p), 1.0, 0.0)
        wx = low_x * (1.0 - fx) + up_x * fx
        sx = up_x - low_x
        v = value[p * ry : (p + 1) * ry]
        g = slope[p * ry : (p + 1) * ry]
        grad_x = grad_x + sx * jnp.sum(wy * v, 0, keepdims=True)
        grad_y = grad_y + wx * jnp.sum(sy * v, 0, keepdims=True)
        grad_z = grad_z + wx * jnp.sum(wy * g, 0, keepdims=True)
    gradient = jnp.concatenate([grad_x, grad_y, grad_z], 0)

    sums = jnp.transpose(acc[...])
    sums = sums[0:8] + sums[8:16] + sums[16:24]
    here = pos[OWN][0:3]
    pair = (SPREAD * charge) * (here * sums[3:4] - sums[0:3])
    old_velocity = velocity[:, 0, 0, :] if first else velocity[...]
    new_velocity = old_velocity + TIME_STEP * (pair - gradient) / mass[...]
    new_moved = TIME_STEP * new_velocity
    if not first:
        new_moved = moved[...] + new_moved
    if last:
        live = lax.broadcasted_iota(jnp.int32, (3, atoms), 1) < own_live
        vel_out[:, 0, 0, :] = jnp.where(live, new_velocity, 0.0)
        moved_out[:, 0, 0, :] = jnp.where(live, new_moved, 0.0)
    else:
        vel_out[...] = new_velocity
        moved_out[...] = new_moved
        next_fraction[...] = own[3:6] + TIME_STEP * new_velocity


def step_call(first, last, sizes, operands, out_shape):
    bx, by, gz, n_x, n_y, atoms = sizes
    scratch = [
        pltpu.VMEM((SLOTS, 8, atoms), F32),
        pltpu.VMEM((SLOTS, 8, atoms), F32),
        pltpu.VMEM((SLOTS, 32, atoms), F32),
        pltpu.VMEM((4, atoms, 128), F32),
        pltpu.VMEM((atoms, 32), F32),
        pltpu.VMEM((bx + 5, by + 8, gz), F32),
        pltpu.VMEM((atoms, 256), BF16),
        pltpu.VMEM((32, 256), BF16),
        pltpu.VMEM((atoms, 512), BF16),
        pltpu.VMEM((32, 512), BF16),
    ]
    if first:
        scratch.append(pltpu.VMEM((bx + 13, by + 16, gz), F32))
    return pl.pallas_call(
        functools.partial(step_kernel, first, last, bx, by, gz, n_x, n_y),
        out_shape=out_shape,
        in_specs=[SMEM, SMEM] + [VMEM] * (len(operands) - 2),
        out_specs=[VMEM] * len(out_shape),
        scratch_shapes=scratch,
        name="first_step" if first else "last_step",
    )(*operands)


def per_device(fraction, velocity, anchor, atom_types, counts, type_table, target):
    atoms = fraction.shape[3]
    bx, by, gz = target.shape
    n_x = bx * lax.axis_size("cells")
    n_y = by * lax.axis_size("grp")
    packet, mass, _, packets, wide, near_counts = exchange(
        (fraction, anchor, atom_types, counts, type_table, target),
        [VMEM, VMEM, VMEM, SMEM, SMEM, ANY],
        [
            jax.ShapeDtypeStruct((8, atoms), F32),
            jax.ShapeDtypeStruct((1, atoms), F32),
            jax.ShapeDtypeStruct((1, 128), F32),
            jax.ShapeDtypeStruct((SLOTS, 8, atoms), F32),
            jax.ShapeDtypeStruct((bx + 13, by + 16, gz), F32),
            jax.ShapeDtypeStruct((SLOTS, 1, 128), F32),
        ],
        [VMEM, VMEM, VMEM, ANY, ANY, ANY],
        bx, by, 0,
    )
    sizes = (bx, by, gz, n_x, n_y, atoms)
    row = jax.ShapeDtypeStruct((3, atoms), F32)
    final = jax.ShapeDtypeStruct(velocity.shape, F32)
    field = jax.ShapeDtypeStruct((bx, by, gz), F32)
    region = jax.ShapeDtypeStruct((bx + 5, by + 8, gz), F32)
    velocity, moved, moved_on, inverse, near = step_call(
        True, False, sizes,
        (counts, near_counts, packets, packet, mass, velocity, wide, target),
        [row, row, row, region, region],
    )
    (later,) = exchange(
        (moved_on,), [ANY], [jax.ShapeDtypeStruct((SLOTS, 3, atoms), F32)], [ANY], bx, by, 1
    )
    return tuple(
        step_call(
            False, True, sizes,
            (counts, near_counts, packets, packet, mass, later, moved_on, velocity, moved, inverse, near),
            [final, final, field],
        )
    )


def solution(mesh):
    placed = (
        P(None, "cells", "grp", None),
        P(None, "cells", "grp", None),
        P(None, "cells", "grp", None),
        P("cells", "grp", None),
        P("cells", "grp"),
        P(),
        P("cells", "grp", None),
    )
    return jax.shard_map(
        per_device,
        mesh=mesh,
        in_specs=placed,
        out_specs=(
            P(None, "cells", "grp", None),
            P(None, "cells", "grp", None),
            P("cells", "grp", None),
        ),
        check_vma=False,
    )
```
